32 devices in a mesh: pen: 16 (over z, x, core), coil: 2 (over y).
Axes of the slice: x: 2, y: 2, z: 4, core: 2. Of those that a mesh axis runs over, the one named last changes fastest.
Arguments:
- image_field: float32 [512, 512, 2, 128], P('pen'), may hold values from -6 to 6
- coil_maps: bfloat16 [2, 512, 512, 2, 128], P('coil', 'pen'), may hold values from -5 to 5
- samples: bfloat16 [2, 4096, 128, 2, 128], P('coil', 'pen'), may hold values from -6 to 6
- kernels: bfloat16 [4096, 128, 128], P('pen'), may hold values from -0.5 to 0.5
- tile_of_block: int32 [4096], P('pen'), may hold values from 0 to 2047, as said below
Outputs:
- gradient: float32 [512, 512, 2, 128], P('pen', 'coil')
The draws below stay inside these ranges and needn't reach their ends.
Inputs may be any that keep to these rules, and one draw needn't show every extreme that they name: The tile of every block lies with the block: tile_of_block[b] // 128 == b // 256; every tile is named by at least one block.
All inputs are finite; a program needn't handle non-finite values.
Results may differ from the reference program's by a relative error of at most 0.012.
Values may be sent and summed in bfloat16 or wider, within the bound.
No kernel may reach another device: no remote copies, remote signals or barrier semaphores. Data moves between devices by JAX's collectives and lax.ppermute only.
A program may use at most 256 MiB of HBM per device.

```python
import jax
import jax.numpy as jnp
from jax import lax

NL = 512
NZ = 128
TILE = 128
SAMP = 128
COILS = 2
LT = 128
TILES = 2048
BLK_DEV = 256
NBLK = 4096


def draw_tile_of_block(key, part):
    dev_count = NBLK // BLK_DEV
    first_key = jax.random.fold_in(key, 11)
    second_key = jax.random.fold_in(key, 12)
    base_tiles = jnp.tile(jnp.arange(LT, dtype=jnp.int32)[None, :], (dev_count, 1))
    extra_tiles = jax.random.randint(first_key, (dev_count, BLK_DEV - LT), 0, LT, dtype=jnp.int32)
    all_tiles = jnp.concatenate([base_tiles, extra_tiles], 1)
    key_list = jax.random.split(second_key, dev_count)
    shuffle = jax.vmap(lambda one_key: jax.random.permutation(one_key, BLK_DEV))(key_list)
    mixed = jnp.take_along_axis(all_tiles, shuffle.astype(jnp.int32), 1)
    owners = jnp.arange(dev_count, dtype=jnp.int32)[:, None] * LT
    return (mixed + owners).reshape(NBLK).astype(jnp.int32)


def shard_levels(stream_key, extent, cuts, least, top_value):
    def one(dim, shards_of):
        draws = jax.random.uniform(jax.random.fold_in(jax.random.fold_in(stream_key, 6), dim), (shards_of,), jnp.float32, least / len(cuts), top_value / len(cuts))
        return jnp.repeat(jnp.exp(draws), extent[dim] // shards_of).reshape((-1,) + (1,) * (len(extent) - dim - 1))

    gain = one(*cuts[0])
    for cut in cuts[1:]:
        gain = gain * one(*cut)
    return gain


def scatter_about(own_key, dims, deviation, limit, pieces=(), kind=jnp.bfloat16):
    level = shard_levels(own_key, dims, pieces, -0.22, 0.18) if pieces else 1.0
    array = jax.random.normal(own_key, dims, jnp.float32) * deviation * level
    return jnp.minimum(jnp.maximum(array, -limit), limit).astype(kind)


def setup_inputs(seed: int = 0) -> dict:
    keys = jax.random.split(jax.random.key(seed), 6)
    return {
        "image_field": scatter_about(keys[0], (NL, NL, 2, NZ), 1.0, 6.0, ((0, 16),), jnp.float32),
        "coil_maps": scatter_about(keys[1], (COILS, NL, NL, 2, NZ), 0.7, 5.0, ((0, 2), (1, 16))),
        "samples": scatter_about(keys[2], (COILS, NBLK, SAMP, 2, NZ), 1.0, 6.0, ((0, 2), (1, 16))),
        "kernels": scatter_about(keys[3], (NBLK, SAMP, TILE), TILE ** -0.5, 0.5, ((0, 16),)),
        "tile_of_block": draw_tile_of_block(jax.random.fold_in(keys[5], 71), 0),
    }


tv_weight = 2.0

def spectrum(real_part, imag_part, axis, inverse):
    values = lax.complex(real_part, imag_part)
    if inverse:
        result = jnp.fft.ifft(values, axis=axis, norm='ortho')
    else:
        result = jnp.fft.fft(values, axis=axis, norm='ortho')
    return (jnp.real(result), jnp.imag(result))

def to_tiles(field):
    return field.reshape(NL // TILE, TILE, NL, 2 * NZ).transpose(2, 0, 1, 3).reshape(TILES, TILE, 2 * NZ)

def from_tiles(tiles):
    return tiles.reshape(NL, NL // TILE, TILE, 2 * NZ).transpose(1, 2, 0, 3).reshape(NL, NL, 2, NZ)

def forward_diff(field, axis):
    count = field.shape[axis]
    head = lax.slice_in_dim(field, 1, count, axis=axis) - lax.slice_in_dim(field, 0, count - 1, axis=axis)
    return jnp.concatenate([head, jnp.zeros_like(lax.slice_in_dim(field, 0, 1, axis=axis))], axis)

def backward_take(flux, axis):
    count = flux.shape[axis]
    before = jnp.concatenate([jnp.zeros_like(lax.slice_in_dim(flux, 0, 1, axis=axis)), lax.slice_in_dim(flux, 0, count - 1, axis=axis)], axis)
    return before - flux

def tv_gradient(field):
    diff_y = forward_diff(field, 0)
    diff_x = forward_diff(field, 1)
    diff_z = forward_diff(field, 3)
    norm_den = jnp.sqrt(1.0 + lax.optimization_barrier(jnp.sum(diff_y * diff_y + diff_x * diff_x + diff_z * diff_z, axis=2, keepdims=True)))
    return backward_take(diff_y / norm_den, 0) + backward_take(diff_x / norm_den, 1) + backward_take(diff_z / norm_den, 3)

def reference(image_field, coil_maps, samples, kernels, tile_of_block):
    field_real = image_field[:, :, 0]
    field_imag = image_field[:, :, 1]
    groups = NBLK // BLK_DEV
    ker_groups = kernels.reshape(groups, BLK_DEV, SAMP, TILE)
    id_groups = tile_of_block.reshape(groups, BLK_DEV)
    summed = jnp.zeros(image_field.shape, jnp.float32)
    for coil_idx in range(COILS):
        map_real = coil_maps[coil_idx, :, :, 0].astype(jnp.float32)
        map_imag = coil_maps[coil_idx, :, :, 1].astype(jnp.float32)
        coil_real = (map_real * field_real - map_imag * field_imag).astype(jnp.bfloat16)
        coil_imag = (map_real * field_imag + map_imag * field_real).astype(jnp.bfloat16)
        spec_real, spec_imag = spectrum(coil_real.astype(jnp.float32), coil_imag.astype(jnp.float32), 1, False)
        spec_real = spec_real.astype(jnp.bfloat16).astype(jnp.float32)
        spec_imag = spec_imag.astype(jnp.bfloat16).astype(jnp.float32)
        grid_real, grid_imag = spectrum(spec_real, spec_imag, 0, False)
        kspace_grid = jnp.stack([grid_real, grid_imag], 2).astype(jnp.bfloat16)
        grid_tiles = to_tiles(kspace_grid)
        sample_groups = samples[coil_idx].reshape(groups, BLK_DEV, SAMP, 2 * NZ)

        def add_group(carry, group):
            ker_block, id_block, sample_block = group
            ker_wide = ker_block.astype(jnp.float32)
            picked = grid_tiles[id_block].astype(jnp.float32)
            predicted = jnp.einsum('bst,btc->bsc', ker_wide, picked)
            misfit = (predicted - sample_block.astype(jnp.float32)).astype(jnp.bfloat16)
            back_terms = jnp.einsum('bst,bsc->btc', ker_wide, misfit.astype(jnp.float32))
            return (carry.at[id_block].add(back_terms), None)
        back_tiles, unused = lax.scan(add_group, jnp.zeros((TILES, TILE, 2 * NZ), jnp.float32), (ker_groups, id_groups, sample_groups))
        back_grid = from_tiles(back_tiles.astype(jnp.bfloat16)).astype(jnp.float32)
        rows_real, rows_imag = spectrum(back_grid[:, :, 0], back_grid[:, :, 1], 0, True)
        rows_real = rows_real.astype(jnp.bfloat16).astype(jnp.float32)
        rows_imag = rows_imag.astype(jnp.bfloat16).astype(jnp.float32)
        back_real, back_imag = spectrum(rows_real, rows_imag, 1, True)
        summed = summed + jnp.stack([map_real * back_real + map_imag * back_imag, map_real * back_imag - map_imag * back_real], 2)
    return summed + tv_weight * tv_gradient(image_field)
```

```python
import functools
import math

import numpy

import jax
import jax.numpy as jnp
from jax import lax
from jax.experimental import pallas as pl
from jax.experimental.pallas import tpu as pltpu

from jax.sharding import PartitionSpec as P

NL = 512
NZ = 128
TILE = 128


tv_weight = 2.0


def shifted(shard, axis, by):
    length = lax.axis_size(axis)
    pairs = [(i, i + by) for i in range(length) if 0 <= i + by < length]
    return lax.ppermute(shard, axis, pairs)


def dft_tables(length, direction):
    index = lax.iota(jnp.int32, length)
    phase = index[:, None] * index[None, :] % length
    angle = 2.0 * math.pi / length * phase.astype(jnp.float32)
    cosine = jnp.cos(angle) / math.sqrt(length)
    sine = direction * jnp.sin(angle) / math.sqrt(length)
    table = jnp.stack([jnp.stack([cosine, sine], -1), jnp.stack([-sine, cosine], -1)], 1)
    high_part = table.astype(jnp.bfloat16)
    low_part = (table - high_part.astype(jnp.float32)).astype(jnp.bfloat16)
    return (high_part, low_part)


def along_second(tables, values):
    first = jnp.einsum("kpxr,yxrz->ykpz", tables[0], values, preferred_element_type=jnp.float32)
    return first + jnp.einsum(
        "kpxr,yxrz->ykpz", tables[1], values, preferred_element_type=jnp.float32
    )


def along_first(tables, values):
    first = jnp.einsum("kpyr,yxrz->kxpz", tables[0], values, preferred_element_type=jnp.float32)
    return first + jnp.einsum(
        "kpyr,yxrz->kxpz", tables[1], values, preferred_element_type=jnp.float32
    )


def flux_fields(extended, first_row, first_col):
    center = extended[:-1, :-1]
    row_ids = first_row + jnp.arange(center.shape[0])
    col_ids = first_col + jnp.arange(center.shape[1])
    diff_y = (extended[1:, :-1] - center) * (row_ids != NL - 1)[:, None, None, None]
    diff_x = (extended[:-1, 1:] - center) * (col_ids != NL - 1)[None, :, None, None]
    diff_z = jnp.concatenate(
        [center[..., 1:] - center[..., :-1], jnp.zeros_like(center[..., :1])], 3
    )
    norm_den = jnp.sqrt(
        1.0 + jnp.sum(diff_y * diff_y + diff_x * diff_x + diff_z * diff_z, axis=2, keepdims=True)
    )
    inside = ((row_ids >= 0)[:, None] & (col_ids >= 0)[None, :]).astype(jnp.float32)[
        :, :, None, None
    ]
    return (diff_y / norm_den * inside, diff_x / norm_den * inside, diff_z / norm_den * inside)


def plane_divergence(flux_z):
    return jnp.concatenate([jnp.zeros_like(flux_z[..., :1]), flux_z[..., :-1]], 3) - flux_z


def on_device(image_field, coil_maps, samples, kernels, tile_of_block):
    own_rows = image_field.shape[0]
    pen_count = lax.axis_size("pen")
    half_cols = NL // lax.axis_size("coil")
    local_cols = NL // pen_count
    pen_id = lax.axis_index("pen")
    coil_id = lax.axis_index("coil")
    row_start = pen_id * own_rows
    col_start = coil_id * half_cols
    map_real = coil_maps[0, :, :, 0].astype(jnp.float32)
    map_imag = coil_maps[0, :, :, 1].astype(jnp.float32)
    field_real = image_field[:, :, 0]
    field_imag = image_field[:, :, 1]
    coil_image = jnp.stack(
        [
            map_real * field_real - map_imag * field_imag,
            map_real * field_imag + map_imag * field_real,
        ],
        2,
    ).astype(jnp.bfloat16)
    forward_tab = dft_tables(NL, 1.0)
    adjoint_tab = dft_tables(NL, -1.0)
    rows_spectrum = along_second(forward_tab, coil_image).astype(jnp.bfloat16)
    kspace_grid = along_first(
        forward_tab, lax.all_to_all(rows_spectrum, "pen", split_axis=1, concat_axis=0, tiled=True)
    ).astype(jnp.bfloat16)
    grid_tiles = (
        kspace_grid.reshape(NL // TILE, TILE, local_cols, 2 * NZ)
        .transpose(2, 0, 1, 3)
        .reshape(-1, TILE, 2 * NZ)
    )
    tile_count = grid_tiles.shape[0]
    local_ids = tile_of_block - pen_id * tile_count
    picked = jnp.take(grid_tiles, local_ids, axis=0)
    predicted = jnp.einsum("bst,btc->bsc", kernels, picked, preferred_element_type=jnp.float32)
    measured = samples[0].reshape(predicted.shape).astype(jnp.float32)
    misfit = (predicted - measured).astype(jnp.bfloat16)
    back_terms = jnp.einsum("bst,bsc->btc", kernels, misfit, preferred_element_type=jnp.float32)
    onehot = (local_ids[:, None] == jnp.arange(tile_count, dtype=jnp.int32)[None, :]).astype(
        jnp.float32
    )
    back_tiles = jnp.einsum(
        "bl,btc->ltc", onehot, back_terms, precision=lax.Precision.HIGHEST
    ).astype(jnp.bfloat16)
    back_grid = (
        back_tiles.reshape(local_cols, NL // TILE, TILE, 2 * NZ)
        .transpose(1, 2, 0, 3)
        .reshape(NL, local_cols, 2, NZ)
    )
    back_rows = along_first(adjoint_tab, back_grid).astype(jnp.bfloat16)
    back_image = along_second(
        adjoint_tab, lax.all_to_all(back_rows, "pen", split_axis=0, concat_axis=1, tiled=True)
    )
    back_real = back_image[:, :, 0]
    back_imag = back_image[:, :, 1]
    coil_term = jnp.stack(
        [map_real * back_real + map_imag * back_imag, map_real * back_imag - map_imag * back_real],
        2,
    )
    summed = lax.psum(coil_term, "coil")
    data_gradient = lax.dynamic_slice_in_dim(summed, col_start, half_cols, 1)
    padded = jnp.pad(image_field, ((0, 0), (1, 1), (0, 0), (0, 0)))
    window = lax.dynamic_slice_in_dim(padded, col_start, half_cols + 2, 1)
    upper_row = shifted(window[:1], "pen", -1)
    extended = jnp.concatenate([window, upper_row], 0)
    flux_y, flux_x, flux_z = flux_fields(extended, row_start, col_start - 1)
    lower_row = shifted(flux_y[-1:], "pen", 1)
    flux_before = jnp.concatenate([lower_row, flux_y[:-1]], 0)
    tv_part = (
        flux_before[:, 1:]
        - flux_y[:, 1:]
        + flux_x[:, :-1]
        - flux_x[:, 1:]
        + plane_divergence(flux_z[:, 1:])
    )
    return data_gradient + tv_weight * tv_part


def pair_tables(scale, row_order, col_order):
    phase = numpy.outer(row_order, col_order) % NL
    angle = 2.0 * math.pi / NL * phase
    return (
        jnp.asarray(numpy.cos(angle) * scale, jnp.bfloat16),
        jnp.asarray(numpy.sin(angle) * scale, jnp.bfloat16),
    )


def mxu(left, right):
    return jnp.dot(left, right, preferred_element_type=jnp.float32)


def rows_kernel(image_ref, maps_ref, cos_ref, sin_ref, out_ref, map_scr, spec_scr):
    half = pl.program_id(1)
    out_rows = cos_ref.shape[0]
    cosine = cos_ref[...]
    sine = sin_ref[...]
    for pair in range(4):
        reals, imags = [], []
        for row in (2 * pair, 2 * pair + 1):
            map_scr[row] = maps_ref[row].astype(jnp.float32)
            map_real = map_scr[row, pl.ds(0, NL, 2), :]
            map_imag = map_scr[row, pl.ds(1, NL, 2), :]
            field_real = image_ref[row, pl.ds(0, NL, 2), :]
            field_imag = image_ref[row, pl.ds(1, NL, 2), :]
            reals.append((map_real * field_real - map_imag * field_imag).astype(jnp.bfloat16))
            imags.append((map_real * field_imag + map_imag * field_real).astype(jnp.bfloat16))
        real = jnp.concatenate(reals, 1)
        imag = jnp.concatenate(imags, 1)
        spec_real = mxu(cosine, real) + mxu(sine, imag)
        spec_imag = mxu(cosine, imag) - mxu(sine, real)
        for sub in range(2):
            base = pl.multiple_of((half * 8 + 2 * pair + sub) * 2 * out_rows, 2 * out_rows)
            lanes = slice(sub * NZ, (sub + 1) * NZ)
            spec_scr[pl.ds(base, out_rows), :] = spec_real[:, lanes]
            spec_scr[pl.ds(base + out_rows, out_rows), :] = spec_imag[:, lanes]

    @pl.when(half == 1)
    def _():
        def move(step, carry):
            for sub in range(8):
                col = step * 8 + sub
                for part in range(2):
                    start = part * out_rows + col
                    low = spec_scr[pl.ds(start, 8, 2 * out_rows), :]
                    high = spec_scr[pl.ds(start + 16 * out_rows, 8, 2 * out_rows), :]
                    out_ref[2 * col + part] = jnp.concatenate([low, high], 0).astype(jnp.bfloat16)
            return carry

        lax.fori_loop(0, out_rows // 8, move, 0)


def row_spectra(image, maps, tables, chunk, chunks):
    rows = image.shape[0]
    out_rows = NL // chunks
    return pl.pallas_call(
        rows_kernel,
        grid=(rows // 16, 2),
        in_specs=[
            pl.BlockSpec((8, 2 * NL, NZ), lambda i, h: (2 * i + h, 0, 0)),
            pl.BlockSpec((8, 2 * NL, NZ), lambda i, h: (2 * i + h, 0, 0)),
            pl.BlockSpec((out_rows, NL), lambda i, h: (chunk, 0)),
            pl.BlockSpec((out_rows, NL), lambda i, h: (chunk, 0)),
        ],
        out_specs=pl.BlockSpec((2 * out_rows, 16, NZ), lambda i, h: (0, i, 0)),
        out_shape=jax.ShapeDtypeStruct((2 * out_rows, rows, NZ), jnp.bfloat16),
        scratch_shapes=[
            pltpu.VMEM((8, 2 * NL, NZ), jnp.float32),
            pltpu.VMEM((16 * 2 * out_rows, NZ), jnp.float32),
        ],
        cost_estimate=pl.CostEstimate(
            flops=8 * rows * out_rows * NL * NZ, bytes_accessed=30000000, transcendentals=0
        ),
    )(image, maps, *tables)


DEPTH = 8


def columns_kernel(
    first_group,
    order_ref,
    local_ref,
    bounds_ref,
    spec_ref,
    cos_ref,
    sin_ref,
    kernels_ref,
    samples_ref,
    *rest,
):
    row_chunks = len(rest) - 10
    outs = rest[:row_chunks]
    tiles, sums, backs, sample_scr, moved, kernel_buf, sample_buf, kernel_sem, sample_sem, _ = rest[
        row_chunks:
    ]
    step = pl.program_id(0)
    steps = pl.num_programs(0)
    first = bounds_ref[first_group]
    last = bounds_ref[first_group + steps]
    begin = bounds_ref[first_group + step]
    end = bounds_ref[first_group + step + 1]

    def fetch(place):
        slot = lax.rem(place, DEPTH)
        block = order_ref[place]
        return (
            pltpu.make_async_copy(kernels_ref.at[block], kernel_buf.at[slot], kernel_sem.at[slot]),
            pltpu.make_async_copy(samples_ref.at[block], sample_buf.at[slot], sample_sem.at[slot]),
        )

    def start(place):
        @pl.when(place < last)
        def _():
            for copy in fetch(place):
                copy.start()

    @pl.when(step == 0)
    def _():
        for ahead in range(DEPTH):
            start(first + ahead)

    cosine = cos_ref[...]
    sine = sin_ref[...]
    length = spec_ref.shape[0] * spec_ref.shape[2]
    parts = [
        jnp.concatenate([spec_ref[:, 2 * col + part].reshape(length, NZ) for col in range(2)], 1)
        for part in range(2)
    ]
    grid_real = (mxu(cosine, parts[0]) + mxu(sine, parts[1])).astype(jnp.bfloat16)
    grid_imag = (mxu(cosine, parts[1]) - mxu(sine, parts[0])).astype(jnp.bfloat16)
    per_col = NL // TILE
    for col in range(2):
        lanes = slice(col * NZ, (col + 1) * NZ)
        for tile in range(per_col):
            cells = slice(tile * TILE, (tile + 1) * TILE)
            tiles[col * per_col + tile, :, :NZ] = grid_real[cells, lanes]
            tiles[col * per_col + tile, :, NZ:] = grid_imag[cells, lanes]
    sums[...] = jnp.zeros_like(sums)

    def one(place, buf):
        slot = lax.rem(place, DEPTH)
        tile = local_ref[place]
        weights = kernel_buf[slot]
        predicted = mxu(weights, tiles[tile])
        sample_scr[buf] = sample_buf[slot].astype(jnp.float32)
        measured = jnp.concatenate(
            [sample_scr[buf, pl.ds(0, TILE, 2), :], sample_scr[buf, pl.ds(1, TILE, 2), :]], 1
        )
        misfit = (predicted - measured).astype(jnp.bfloat16)
        back = lax.dot_general(
            weights, misfit, (((0,), (0,)), ((), ())), preferred_element_type=jnp.float32
        )
        return tile, back

    def two(pair, carry):
        place = begin + 2 * pair
        other = jnp.minimum(place + 1, end - 1)
        for copy in fetch(place):
            copy.wait()

        @pl.when(place + 1 < end)
        def _():
            for copy in fetch(place + 1):
                copy.wait()

        tile_a, back_a = one(place, 0)
        tile_b, back_b = one(other, 1)
        sums[tile_a] += back_a
        sums[tile_b] += jnp.where(place + 1 < end, back_b, 0.0)
        start(place + DEPTH)

        @pl.when(place + 1 < end)
        def _():
            start(place + 1 + DEPTH)

        return carry

    lax.fori_loop(0, (end - begin + 1) // 2, two, 0)

    for col in range(2):
        lanes = slice(col * NZ, (col + 1) * NZ)
        for tile in range(per_col):
            cells = slice(tile * TILE, (tile + 1) * TILE)
            value = sums[col * per_col + tile].astype(jnp.bfloat16)
            backs[0, cells, lanes] = value[:, :NZ]
            backs[1, cells, lanes] = value[:, NZ:]
    back_real = backs[0]
    back_imag = backs[1]
    rows_real = mxu(cosine, back_real) - mxu(sine, back_imag)
    rows_imag = mxu(sine, back_real) + mxu(cosine, back_imag)
    for col in range(2):
        lanes = slice(col * NZ, (col + 1) * NZ)
        base = pl.multiple_of((2 * step + col) * 2 * NL, 2 * NL)
        moved[pl.ds(base, NL), :] = rows_real[:, lanes]
        moved[pl.ds(base + NL, NL), :] = rows_imag[:, lanes]

    @pl.when(step == steps - 1)
    def _():
        owners, own_rows = spec_ref.shape[0], spec_ref.shape[2]
        each = own_rows // row_chunks
        groups = moved.shape[0] // (16 * NL)
        for piece in range(row_chunks):

            def move(row, carry):
                owner = row // each
                source = owner * own_rows + piece * each + lax.rem(row, each)
                for part in range(2):
                    start_row = part * NL + source
                    outs[piece][2 * row + part] = jnp.concatenate(
                        [
                            moved[pl.ds(start_row + 16 * NL * group, 8, 2 * NL), :]
                            for group in range(groups)
                        ],
                        0,
                    ).astype(jnp.bfloat16)
                return carry

            lax.fori_loop(0, owners * each, move, 0, unroll=4)


def column_stage(spectra, tables, kernels, samples, plan, chunk, chunks, row_chunks):
    owners, width, own_rows = spectra.shape[:3]
    steps = width // 4
    per_col = NL // TILE
    cols = width // 2
    each = own_rows // row_chunks
    whole = lambda i, *refs: (0, 0)
    return pl.pallas_call(
        functools.partial(columns_kernel, chunk * steps),
        grid_spec=pltpu.PrefetchScalarGridSpec(
            num_scalar_prefetch=3,
            grid=(steps,),
            in_specs=[
                pl.BlockSpec((owners, 4, own_rows, NZ), lambda i, *refs: (0, i, 0, 0)),
                pl.BlockSpec((NL, NL), whole),
                pl.BlockSpec((NL, NL), whole),
                pl.BlockSpec(memory_space=pl.ANY),
                pl.BlockSpec(memory_space=pl.ANY),
            ],
            out_specs=[
                pl.BlockSpec((owners * each * 2, cols, NZ), lambda i, *refs: (0, 0, 0))
                for _ in range(row_chunks)
            ],
            scratch_shapes=[
                pltpu.VMEM((2 * per_col, TILE, 2 * NZ), jnp.bfloat16),
                pltpu.VMEM((2 * per_col, TILE, 2 * NZ), jnp.float32),
                pltpu.VMEM((2, NL, 2 * NZ), jnp.bfloat16),
                pltpu.VMEM((2, 2 * TILE, NZ), jnp.float32),
                pltpu.VMEM((cols * 2 * NL, NZ), jnp.float32),
                pltpu.VMEM((DEPTH, TILE, TILE), jnp.bfloat16),
                pltpu.VMEM((DEPTH, 2 * TILE, NZ), jnp.bfloat16),
                pltpu.SemaphoreType.DMA((DEPTH,)),
                pltpu.SemaphoreType.DMA((DEPTH,)),
                pltpu.VMEM((8, NZ), jnp.float32),
            ],
        ),
        out_shape=[
            jax.ShapeDtypeStruct((owners * each * 2, cols, NZ), jnp.bfloat16)
            for _ in range(row_chunks)
        ],
        cost_estimate=pl.CostEstimate(
            flops=60000000000 // chunks, bytes_accessed=40000000 // chunks, transcendentals=0
        ),
    )(*plan, spectra, *tables, kernels, samples)


def image_kernel(coil_ref, early_ref, late_ref, maps_ref, cos_ref, sin_ref, own_ref, send_ref, map_scr):
    coil_id = coil_ref[0]
    cosine = cos_ref[...]
    sine = sin_ref[...]
    count = early_ref.shape[0] * early_ref.shape[3]
    half = NL // 2
    parts = []
    for part in range(2):
        lanes = []
        for row in range(2):
            lanes.append(
                jnp.concatenate(
                    [
                        early_ref[:, row, part].reshape(count, NZ),
                        late_ref[:, row, part].reshape(count, NZ),
                    ],
                    0,
                )
            )
        parts.append(jnp.concatenate(lanes, 1))
    back_real = mxu(cosine, parts[0]) - mxu(sine, parts[1])
    back_imag = mxu(sine, parts[0]) + mxu(cosine, parts[1])
    for row in range(2):
        lanes = slice(row * NZ, (row + 1) * NZ)
        for which in range(2):
            rows = slice(which * half, (which + 1) * half)
            side = coil_id if which == 0 else 1 - coil_id
            map_scr[2 * row + which] = maps_ref[row, side].astype(jnp.float32)
            map_real = map_scr[2 * row + which, pl.ds(0, half, 2), :]
            map_imag = map_scr[2 * row + which, pl.ds(1, half, 2), :]
            real = back_real[rows, lanes]
            imag = back_imag[rows, lanes]
            term_real = map_real * real + map_imag * imag
            term_imag = map_real * imag - map_imag * real
            if which == 0:
                own_ref[row, 0] = term_real
                own_ref[row, 1] = term_imag
            else:
                send_ref[row, 0] = term_real.astype(jnp.bfloat16)
                send_ref[row, 1] = term_imag.astype(jnp.bfloat16)


def image_stage(coil_id, early, late, maps, tables, piece):
    owners, each, _, cols = late.shape[:4]
    half = NL // 2
    base = piece * each // 2
    whole = lambda i, *refs: (0, 0)
    return pl.pallas_call(
        image_kernel,
        grid_spec=pltpu.PrefetchScalarGridSpec(
            num_scalar_prefetch=1,
            grid=(each // 2,),
            in_specs=[
                pl.BlockSpec((owners, 2, 2, cols, NZ), lambda i, *refs: (0, base + i, 0, 0, 0)),
                pl.BlockSpec((owners, 2, 2, cols, NZ), lambda i, *refs: (0, i, 0, 0, 0)),
                pl.BlockSpec((2, 2, NL, NZ), lambda i, *refs: (base + i, 0, 0, 0)),
                pl.BlockSpec((NL, NL), whole),
                pl.BlockSpec((NL, NL), whole),
            ],
            out_specs=[
                pl.BlockSpec((2, 2, half, NZ), lambda i, *refs: (i, 0, 0, 0)),
                pl.BlockSpec((2, 2, half, NZ), lambda i, *refs: (i, 0, 0, 0)),
            ],
            scratch_shapes=[pltpu.VMEM((4, NL, NZ), jnp.float32)],
        ),
        out_shape=[
            jax.ShapeDtypeStruct((each, 2, half, NZ), jnp.float32),
            jax.ShapeDtypeStruct((each, 2, half, NZ), jnp.bfloat16),
        ],
        cost_estimate=pl.CostEstimate(
            flops=8 * each * NL * NL * NZ, bytes_accessed=each * 1200000, transcendentals=0
        ),
    )(coil_id, early, late, maps, *tables)


def sum_kernel(total_ref, own_ref, other_ref, out_ref):
    half = own_ref.shape[2]
    for row in range(own_ref.shape[0]):
        for part in range(2):
            rows = pl.ds(part, half, 2)
            out_ref[row, rows, :] = (
                total_ref[row, rows, :] + own_ref[row, part] + other_ref[row, part].astype(jnp.float32)
            )


def sum_stage(total, own, other, piece):
    each, _, half = own.shape[:3]
    rows = 4
    base = piece * each // rows
    return pl.pallas_call(
        sum_kernel,
        grid=(each // rows,),
        in_specs=[
            pl.BlockSpec((rows, 2 * half, NZ), lambda i: (base + i, 0, 0)),
            pl.BlockSpec((rows, 2, half, NZ), lambda i: (i, 0, 0, 0)),
            pl.BlockSpec((rows, 2, half, NZ), lambda i: (i, 0, 0, 0)),
        ],
        out_specs=pl.BlockSpec((rows, 2 * half, NZ), lambda i: (base + i, 0, 0)),
        out_shape=jax.ShapeDtypeStruct(total.shape, jnp.float32),
        input_output_aliases={0: 0},
        cost_estimate=pl.CostEstimate(
            flops=4 * each * half * NZ, bytes_accessed=each * 1000000, transcendentals=0
        ),
    )(total, own, other)


def block_plan(tile_of_block, pen_id, tile_count, group):
    count = tile_of_block.shape[0]
    local = tile_of_block - pen_id * tile_count
    spot = jnp.arange(count, dtype=jnp.int32)
    key = local * count + spot
    rank = jnp.sum((key[None, :] < key[:, None]).astype(jnp.int32), 1)
    hit = (rank[None, :] == spot[:, None]).astype(jnp.int32)
    order = jnp.sum(hit * spot[None, :], 1)
    sorted_tile = jnp.sum(hit * local[None, :], 1)
    edges = jnp.arange(tile_count // group + 1, dtype=jnp.int32) * group
    bounds = jnp.sum((local[None, :] < edges[:, None]).astype(jnp.int32), 1)
    return (order, sorted_tile % group, bounds)


def on_device_fast(*args):
    return gradient_parts(*args)


def gradient_parts(image_field, coil_maps, samples, kernels, tile_of_block):
    own_rows = image_field.shape[0]
    pen_count = lax.axis_size("pen")
    local_cols = NL // pen_count
    pen_id = lax.axis_index("pen")
    coil_id = lax.axis_index("coil")
    chunks, row_chunks = 2, 4
    chunk_cols = local_cols // chunks
    image = image_field.reshape(own_rows, 2 * NL, NZ)
    maps = coil_maps.reshape(own_rows, 2 * NL, NZ)
    block_count = kernels.shape[0]
    sample_rows = samples.reshape(block_count, 2 * TILE, NZ)
    natural = numpy.arange(NL)
    split = (
        natural.reshape(pen_count, chunks, chunk_cols).transpose(1, 0, 2).reshape(NL)
    )
    tables_rows = pair_tables(1.0 / 16, split, natural)
    tables_cols = pair_tables(1.0 / 32, natural, natural)
    tables_back = pair_tables(1.0 / 16, natural, split)
    tables_back = [jnp.roll(table, -coil_id * (NL // 2), 0) for table in tables_back]
    per_col = NL // TILE
    plan = block_plan(tile_of_block, pen_id, block_count // 2, 2 * per_col)

    def exchange(array):
        return lax.all_to_all(array, "pen", split_axis=0, concat_axis=0, tiled=True)

    above = shifted(image[-1:], "pen", 1)
    below = shifted(image[:1], "pen", -1)
    arrived = []
    for chunk in range(chunks):
        spectra = row_spectra(image, maps, tables_rows, chunk, chunks)
        spectra = spectra.reshape(pen_count, 2 * chunk_cols, own_rows, NZ)
        arrived.append(exchange(spectra))
    back = []
    for chunk in range(chunks):
        pieces = 1 if chunk == 0 else row_chunks
        result = column_stage(
            arrived[chunk], tables_cols, kernels, sample_rows, plan, chunk, chunks, pieces
        )
        got = []
        for piece in range(pieces):
            one = result[piece].reshape(pen_count, own_rows // pieces, 2, chunk_cols, NZ)
            got.append(exchange(one))
        back.append(got)
    total = variation_stage(image, above, below, jnp.stack([coil_id, pen_id]).astype(jnp.int32))
    side_maps = maps.reshape(own_rows, 2, NL, NZ)
    coil_vec = coil_id.reshape(1).astype(jnp.int32)
    for piece in range(row_chunks):
        own, send = image_stage(
            coil_vec, back[0][0], back[1][piece], side_maps, tables_back, piece
        )
        other = lax.ppermute(send, "coil", [(0, 1), (1, 0)])
        total = sum_stage(total, own, other, piece)
    return total.reshape(own_rows, NL // 2, 2, NZ)


def variation_kernel(where_ref, rows_ref, after_ref, above_ref, below_ref, out_ref, window, flux_y, flux_x):
    coil_id = where_ref[0]
    pen_id = where_ref[1]
    step = pl.program_id(0)
    steps = pl.num_programs(0)
    count = rows_ref.shape[0]
    half = out_ref.shape[1]
    offset = pl.multiple_of(coil_id * half, half)
    before = pl.multiple_of(jnp.maximum(offset - 8, 0), 8)
    behind = pl.multiple_of(jnp.minimum(offset + half, 2 * NL - 8), 8)
    lane = lax.broadcasted_iota(jnp.int32, (1, NZ), 1)
    not_last_plane = (lane != NZ - 1).astype(jnp.float32)

    def place(slot, ref, row):
        window[slot, pl.ds(0, 8), :] = ref[row, pl.ds(before, 8), :]
        window[slot, pl.ds(8, half), :] = ref[row, pl.ds(offset, half), :]
        window[slot, pl.ds(half + 8, 8), :] = ref[row, pl.ds(behind, 8), :]

    def flux(slot, next_slot, start, size, row_scale):
        center = window[slot, pl.ds(start, size), :]
        row = lax.broadcasted_iota(jnp.int32, (size, NZ), 0)
        column_row = row + (start - 8) + offset
        not_last = jnp.where(column_row < 2 * NL - 2, 1.0, 0.0)
        diff_y = (window[next_slot, pl.ds(start, size), :] - center) * row_scale
        diff_x = (window[slot, pl.ds(start + 2, size), :] - center) * not_last
        diff_z = (pltpu.roll(center, NZ - 1, 1) - center) * not_last_plane
        square = diff_y * diff_y + diff_x * diff_x + diff_z * diff_z
        split = square.reshape(size // 8, 8, NZ)
        up = pltpu.roll(split, 7, 1).reshape(size, NZ)
        down = pltpu.roll(split, 1, 1).reshape(size, NZ)
        square = square + jnp.where(row % 2 == 0, up, down)
        scale = lax.rsqrt(1.0 + square)
        return diff_y * scale, diff_x * scale, diff_z * scale

    size = half // 4

    @pl.when(step == 0)
    def _():
        place(1, above_ref, 0)
        place(0, rows_ref, 0)
        inside = jnp.where(pen_id > 0, 1.0, 0.0)

        def first(part, carry):
            start = pl.multiple_of(8 + part * size, 8)
            flux_y[pl.ds(start - 8, size), :] = flux(1, 0, start, size, 1.0)[0] * inside
            return carry

        lax.fori_loop(0, 4, first, 0)

    last_step = step == steps - 1
    last_pen = pen_id == lax.axis_size("pen") - 1

    def one_row(row, carry):
        slot = lax.rem(row, 2)
        is_end = row == count - 1

        @pl.when(jnp.logical_not(is_end))
        def _():
            place(1 - slot, rows_ref, jnp.minimum(row + 1, count - 1))

        @pl.when(jnp.logical_and(is_end, jnp.logical_not(last_step)))
        def _():
            place(1 - slot, after_ref, 0)

        @pl.when(jnp.logical_and(is_end, last_step))
        def _():
            place(1 - slot, below_ref, 0)

        row_scale = jnp.where(
            jnp.logical_and(jnp.logical_and(is_end, last_step), last_pen), 0.0, 1.0
        )
        edge = flux(slot, 1 - slot, 0, 8, row_scale)[1]
        flux_x[pl.ds(0, 8), :] = edge * jnp.where(coil_id > 0, 1.0, 0.0)

        def part_of(part, carry):
            start = pl.multiple_of(8 + part * size, 8)
            here_y, here_x, here_z = flux(slot, 1 - slot, start, size, row_scale)
            flux_x[pl.ds(start, size), :] = here_x
            past_y = flux_y[pl.ds(start - 8, size), :]
            flux_y[pl.ds(start - 8, size), :] = here_y
            past_x = flux_x[pl.ds(start - 2, size), :]
            past_z = pltpu.roll(here_z, 1, 1)
            total = (past_y - here_y) + (past_x - here_x) + (past_z - here_z)
            out_ref[row, pl.ds(start - 8, size), :] = tv_weight * total
            return carry

        lax.fori_loop(0, 4, part_of, 0)
        return carry

    lax.fori_loop(0, count, one_row, 0)


def variation_stage(image, above, below, where):
    rows = image.shape[0]
    count = 8
    return pl.pallas_call(
        variation_kernel,
        grid_spec=pltpu.PrefetchScalarGridSpec(
            num_scalar_prefetch=1,
            grid=(rows // count,),
            in_specs=[
                pl.BlockSpec((count, 2 * NL, NZ), lambda i, *refs: (i, 0, 0)),
                pl.BlockSpec(
                    (1, 2 * NL, NZ), lambda i, *refs: (jnp.minimum(count * (i + 1), rows - 1), 0, 0)
                ),
                pl.BlockSpec((1, 2 * NL, NZ), lambda i, *refs: (0, 0, 0)),
                pl.BlockSpec((1, 2 * NL, NZ), lambda i, *refs: (0, 0, 0)),
            ],
            out_specs=pl.BlockSpec((count, NL, NZ), lambda i, *refs: (i, 0, 0)),
            scratch_shapes=[
                pltpu.VMEM((2, NL + 16, NZ), jnp.float32),
                pltpu.VMEM((NL, NZ), jnp.float32),
                pltpu.VMEM((NL + 8, NZ), jnp.float32),
            ],
        ),
        out_shape=jax.ShapeDtypeStruct((rows, NL, NZ), jnp.float32),
        cost_estimate=pl.CostEstimate(
            flops=40 * rows * NL * NZ, bytes_accessed=60000000, transcendentals=0
        ),
        name="variation",
    )(where, image, image, above, below)


def solution(mesh):
    in_specs = (
        P("pen", None, None, None),
        P("coil", "pen", None, None, None),
        P("coil", "pen", None, None, None),
        P("pen", None, None),
        P("pen"),
    )
    out_specs = P("pen", "coil", None, None)
    own_rows = NL // mesh.shape["pen"]
    body = on_device_fast if own_rows % 32 == 0 else on_device
    return jax.shard_map(
        body, mesh=mesh, in_specs=in_specs, out_specs=out_specs, check_vma=False
    )
```

```python
import functools
import math

import numpy

import jax
import jax.numpy as jnp
from jax import lax
from jax.experimental import pallas as pl
from jax.experimental.pallas import tpu as pltpu

from jax.sharding import PartitionSpec as P

NL = 512
NZ = 128
TILE = 128


tv_weight = 2.0


def shifted(shard, axis, by):
    length = lax.axis_size(axis)
    pairs = [(i, i + by) for i in range(length) if 0 <= i + by < length]
    return lax.ppermute(shard, axis, pairs)


def dft_tables(length, direction):
    index = lax.iota(jnp.int32, length)
    phase = index[:, None] * index[None, :] % length
    angle = 2.0 * math.pi / length * phase.astype(jnp.float32)
    cosine = jnp.cos(angle) / math.sqrt(length)
    sine = direction * jnp.sin(angle) / math.sqrt(length)
    table = jnp.stack([jnp.stack([cosine, sine], -1), jnp.stack([-sine, cosine], -1)], 1)
    high_part = table.astype(jnp.bfloat16)
    low_part = (table - high_part.astype(jnp.float32)).astype(jnp.bfloat16)
    return (high_part, low_part)


def along_second(tables, values):
    first = jnp.einsum("kpxr,yxrz->ykpz", tables[0], values, preferred_element_type=jnp.float32)
    return first + jnp.einsum(
        "kpxr,yxrz->ykpz", tables[1], values, preferred_element_type=jnp.float32
    )


def along_first(tables, values):
    first = jnp.einsum("kpyr,yxrz->kxpz", tables[0], values, preferred_element_type=jnp.float32)
    return first + jnp.einsum(
        "kpyr,yxrz->kxpz", tables[1], values, preferred_element_type=jnp.float32
    )


def flux_fields(extended, first_row, first_col):
    center = extended[:-1, :-1]
    row_ids = first_row + jnp.arange(center.shape[0])
    col_ids = first_col + jnp.arange(center.shape[1])
    diff_y = (extended[1:, :-1] - center) * (row_ids != NL - 1)[:, None, None, None]
    diff_x = (extended[:-1, 1:] - center) * (col_ids != NL - 1)[None, :, None, None]
    diff_z = jnp.concatenate(
        [center[..., 1:] - center[..., :-1], jnp.zeros_like(center[..., :1])], 3
    )
    norm_den = jnp.sqrt(
        1.0 + jnp.sum(diff_y * diff_y + diff_x * diff_x + diff_z * diff_z, axis=2, keepdims=True)
    )
    inside = ((row_ids >= 0)[:, None] & (col_ids >= 0)[None, :]).astype(jnp.float32)[
        :, :, None, None
    ]
    return (diff_y / norm_den * inside, diff_x / norm_den * inside, diff_z / norm_den * inside)


def plane_divergence(flux_z):
    return jnp.concatenate([jnp.zeros_like(flux_z[..., :1]), flux_z[..., :-1]], 3) - flux_z


def on_device(image_field, coil_maps, samples, kernels, tile_of_block):
    own_rows = image_field.shape[0]
    pen_count = lax.axis_size("pen")
    half_cols = NL // lax.axis_size("coil")
    local_cols = NL // pen_count
    pen_id = lax.axis_index("pen")
    coil_id = lax.axis_index("coil")
    row_start = pen_id * own_rows
    col_start = coil_id * half_cols
    map_real = coil_maps[0, :, :, 0].astype(jnp.float32)
    map_imag = coil_maps[0, :, :, 1].astype(jnp.float32)
    field_real = image_field[:, :, 0]
    field_imag = image_field[:, :, 1]
    coil_image = jnp.stack(
        [
            map_real * field_real - map_imag * field_imag,
            map_real * field_imag + map_imag * field_real,
        ],
        2,
    ).astype(jnp.bfloat16)
    forward_tab = dft_tables(NL, 1.0)
    adjoint_tab = dft_tables(NL, -1.0)
    rows_spectrum = along_second(forward_tab, coil_image).astype(jnp.bfloat16)
    kspace_grid = along_first(
        forward_tab, lax.all_to_all(rows_spectrum, "pen", split_axis=1, concat_axis=0, tiled=True)
    ).astype(jnp.bfloat16)
    grid_tiles = (
        kspace_grid.reshape(NL // TILE, TILE, local_cols, 2 * NZ)
        .transpose(2, 0, 1, 3)
        .reshape(-1, TILE, 2 * NZ)
    )
    tile_count = grid_tiles.shape[0]
    local_ids = tile_of_block - pen_id * tile_count
    picked = jnp.take(grid_tiles, local_ids, axis=0)
    predicted = jnp.einsum("bst,btc->bsc", kernels, picked, preferred_element_type=jnp.float32)
    measured = samples[0].reshape(predicted.shape).astype(jnp.float32)
    misfit = (predicted - measured).astype(jnp.bfloat16)
    back_terms = jnp.einsum("bst,bsc->btc", kernels, misfit, preferred_element_type=jnp.float32)
    onehot = (local_ids[:, None] == jnp.arange(tile_count, dtype=jnp.int32)[None, :]).astype(
        jnp.float32
    )
    back_tiles = jnp.einsum(
        "bl,btc->ltc", onehot, back_terms, precision=lax.Precision.HIGHEST
    ).astype(jnp.bfloat16)
    back_grid = (
        back_tiles.reshape(local_cols, NL // TILE, TILE, 2 * NZ)
        .transpose(1, 2, 0, 3)
        .reshape(NL, local_cols, 2, NZ)
    )
    back_rows = along_first(adjoint_tab, back_grid).astype(jnp.bfloat16)
    back_image = along_second(
        adjoint_tab, lax.all_to_all(back_rows, "pen", split_axis=0, concat_axis=1, tiled=True)
    )
    back_real = back_image[:, :, 0]
    back_imag = back_image[:, :, 1]
    coil_term = jnp.stack(
        [map_real * back_real + map_imag * back_imag, map_real * back_imag - map_imag * back_real],
        2,
    )
    summed = lax.psum(coil_term, "coil")
    data_gradient = lax.dynamic_slice_in_dim(summed, col_start, half_cols, 1)
    padded = jnp.pad(image_field, ((0, 0), (1, 1), (0, 0), (0, 0)))
    window = lax.dynamic_slice_in_dim(padded, col_start, half_cols + 2, 1)
    upper_row = shifted(window[:1], "pen", -1)
    extended = jnp.concatenate([window, upper_row], 0)
    flux_y, flux_x, flux_z = flux_fields(extended, row_start, col_start - 1)
    lower_row = shifted(flux_y[-1:], "pen", 1)
    flux_before = jnp.concatenate([lower_row, flux_y[:-1]], 0)
    tv_part = (
        flux_before[:, 1:]
        - flux_y[:, 1:]
        + flux_x[:, :-1]
        - flux_x[:, 1:]
        + plane_divergence(flux_z[:, 1:])
    )
    return data_gradient + tv_weight * tv_part


def pair_tables(scale, row_order, col_order):
    phase = numpy.outer(row_order, col_order) % NL
    angle = 2.0 * math.pi / NL * phase
    return (
        jnp.asarray(numpy.cos(angle) * scale, jnp.bfloat16),
        jnp.asarray(numpy.sin(angle) * scale, jnp.bfloat16),
    )


def mxu(left, right):
    return jnp.dot(left, right, preferred_element_type=jnp.float32)


def rows_kernel(image_ref, maps_ref, cos_ref, sin_ref, out_ref, map_scr, spec_scr):
    half = pl.program_id(1)
    out_rows = cos_ref.shape[0]
    cosine = cos_ref[...]
    sine = sin_ref[...]
    for pair in range(4):
        reals, imags = [], []
        for row in (2 * pair, 2 * pair + 1):
            map_scr[row] = maps_ref[row].astype(jnp.float32)
            map_real = map_scr[row, pl.ds(0, NL, 2), :]
            map_imag = map_scr[row, pl.ds(1, NL, 2), :]
            field_real = image_ref[row, pl.ds(0, NL, 2), :]
            field_imag = image_ref[row, pl.ds(1, NL, 2), :]
            reals.append((map_real * field_real - map_imag * field_imag).astype(jnp.bfloat16))
            imags.append((map_real * field_imag + map_imag * field_real).astype(jnp.bfloat16))
        real = jnp.concatenate(reals, 1)
        imag = jnp.concatenate(imags, 1)
        spec_real = mxu(cosine, real) + mxu(sine, imag)
        spec_imag = mxu(cosine, imag) - mxu(sine, real)
        for sub in range(2):
            base = pl.multiple_of((half * 8 + 2 * pair + sub) * 2 * out_rows, 2 * out_rows)
            lanes = slice(sub * NZ, (sub + 1) * NZ)
            spec_scr[pl.ds(base, out_rows), :] = spec_real[:, lanes]
            spec_scr[pl.ds(base + out_rows, out_rows), :] = spec_imag[:, lanes]

    @pl.when(half == 1)
    def _():
        def move(step, carry):
            for sub in range(8):
                col = step * 8 + sub
                for part in range(2):
                    start = part * out_rows + col
                    low = spec_scr[pl.ds(start, 8, 2 * out_rows), :]
                    high = spec_scr[pl.ds(start + 16 * out_rows, 8, 2 * out_rows), :]
                    out_ref[2 * col + part] = jnp.concatenate([low, high], 0).astype(jnp.bfloat16)
            return carry

        lax.fori_loop(0, out_rows // 8, move, 0)


def row_spectra(image, maps, tables, chunk, chunks):
    rows = image.shape[0]
    out_rows = NL // chunks
    return pl.pallas_call(
        rows_kernel,
        grid=(rows // 16, 2),
        in_specs=[
            pl.BlockSpec((8, 2 * NL, NZ), lambda i, h: (2 * i + h, 0, 0)),
            pl.BlockSpec((8, 2 * NL, NZ), lambda i, h: (2 * i + h, 0, 0)),
            pl.BlockSpec((out_rows, NL), lambda i, h: (chunk, 0)),
            pl.BlockSpec((out_rows, NL), lambda i, h: (chunk, 0)),
        ],
        out_specs=pl.BlockSpec((2 * out_rows, 16, NZ), lambda i, h: (0, i, 0)),
        out_shape=jax.ShapeDtypeStruct((2 * out_rows, rows, NZ), jnp.bfloat16),
        scratch_shapes=[
            pltpu.VMEM((8, 2 * NL, NZ), jnp.float32),
            pltpu.VMEM((16 * 2 * out_rows, NZ), jnp.float32),
        ],
        cost_estimate=pl.CostEstimate(
            flops=8 * rows * out_rows * NL * NZ, bytes_accessed=30000000, transcendentals=0
        ),
    )(image, maps, *tables)


DEPTH = 8


def columns_kernel(
    first_group,
    jobs,
    order_ref,
    local_ref,
    bounds_ref,
    pen_ref,
    spec_ref,
    cos_ref,
    sin_ref,
    kernels_ref,
    samples_ref,
    *rest,
):
    out_count = len(jobs)
    outs = rest[:out_count]
    tiles, sums, backs, sample_scr, moved, kernel_buf, sample_buf, kernel_sem, sample_sem, _ = rest[
        out_count:
    ]
    step = pl.program_id(0)
    steps = pl.num_programs(0)
    first = bounds_ref[first_group]
    last = bounds_ref[first_group + steps]
    begin = bounds_ref[first_group + step]
    end = bounds_ref[first_group + step + 1]

    def fetch(place):
        slot = lax.rem(place, DEPTH)
        block = order_ref[place]
        return (
            pltpu.make_async_copy(kernels_ref.at[block], kernel_buf.at[slot], kernel_sem.at[slot]),
            pltpu.make_async_copy(samples_ref.at[block], sample_buf.at[slot], sample_sem.at[slot]),
        )

    def start(place):
        @pl.when(place < last)
        def _():
            for copy in fetch(place):
                copy.start()

    @pl.when(step == 0)
    def _():
        for ahead in range(DEPTH):
            start(first + ahead)

    cosine = cos_ref[...]
    sine = sin_ref[...]
    length = spec_ref.shape[0] * spec_ref.shape[2]
    parts = [
        jnp.concatenate([spec_ref[:, 2 * col + part].reshape(length, NZ) for col in range(2)], 1)
        for part in range(2)
    ]
    grid_real = (mxu(cosine, parts[0]) + mxu(sine, parts[1])).astype(jnp.bfloat16)
    grid_imag = (mxu(cosine, parts[1]) - mxu(sine, parts[0])).astype(jnp.bfloat16)
    per_col = NL // TILE
    for col in range(2):
        lanes = slice(col * NZ, (col + 1) * NZ)
        for tile in range(per_col):
            cells = slice(tile * TILE, (tile + 1) * TILE)
            tiles[col * per_col + tile, :, :NZ] = grid_real[cells, lanes]
            tiles[col * per_col + tile, :, NZ:] = grid_imag[cells, lanes]
    sums[...] = jnp.zeros_like(sums)

    def one(place, buf):
        slot = lax.rem(place, DEPTH)
        tile = local_ref[place]
        weights = kernel_buf[slot]
        predicted = mxu(weights, tiles[tile])
        sample_scr[buf] = sample_buf[slot].astype(jnp.float32)
        measured = jnp.concatenate(
            [sample_scr[buf, pl.ds(0, TILE, 2), :], sample_scr[buf, pl.ds(1, TILE, 2), :]], 1
        )
        misfit = (predicted - measured).astype(jnp.bfloat16)
        back = lax.dot_general(
            weights, misfit, (((0,), (0,)), ((), ())), preferred_element_type=jnp.float32
        )
        return tile, back

    def two(pair, carry):
        place = begin + 2 * pair
        other = jnp.minimum(place + 1, end - 1)
        for copy in fetch(place):
            copy.wait()

        @pl.when(place + 1 < end)
        def _():
            for copy in fetch(place + 1):
                copy.wait()

        tile_a, back_a = one(place, 0)
        tile_b, back_b = one(other, 1)
        sums[tile_a] += back_a
        sums[tile_b] += jnp.where(place + 1 < end, back_b, 0.0)
        start(place + DEPTH)

        @pl.when(place + 1 < end)
        def _():
            start(place + 1 + DEPTH)

        return carry

    lax.fori_loop(0, (end - begin + 1) // 2, two, 0)

    for col in range(2):
        lanes = slice(col * NZ, (col + 1) * NZ)
        for tile in range(per_col):
            cells = slice(tile * TILE, (tile + 1) * TILE)
            value = sums[col * per_col + tile].astype(jnp.bfloat16)
            backs[0, cells, lanes] = value[:, :NZ]
            backs[1, cells, lanes] = value[:, NZ:]
    back_real = backs[0]
    back_imag = backs[1]
    rows_real = mxu(cosine, back_real) - mxu(sine, back_imag)
    rows_imag = mxu(sine, back_real) + mxu(cosine, back_imag)
    for col in range(2):
        lanes = slice(col * NZ, (col + 1) * NZ)
        base = pl.multiple_of((2 * step + col) * 2 * NL, 2 * NL)
        moved[pl.ds(base, NL), :] = rows_real[:, lanes]
        moved[pl.ds(base + NL, NL), :] = rows_imag[:, lanes]

    @pl.when(step == steps - 1)
    def _():
        own_rows = spec_ref.shape[2]
        groups = moved.shape[0] // (16 * NL)
        for out, (kind, which, count, base_row, each) in zip(outs, jobs):
            if kind == "cross":
                base_owner = pen_ref[0] ^ which
            elif kind == "near":
                base_owner = pen_ref[0] & which
            else:
                base_owner = 0

            def move(row, carry):
                owner = base_owner + row // each
                source = owner * own_rows + base_row + lax.rem(row, each)
                for part in range(2):
                    start_row = part * NL + source
                    out[2 * row + part] = jnp.concatenate(
                        [
                            moved[pl.ds(start_row + 16 * NL * group, 8, 2 * NL), :]
                            for group in range(groups)
                        ],
                        0,
                    ).astype(jnp.bfloat16)
                return carry

            lax.fori_loop(0, count * each, move, 0, unroll=2)


def column_stage(spectra, tables, kernels, samples, plan, chunk, chunks, jobs):
    owners, width, own_rows = spectra.shape[:3]
    steps = width // 4
    per_col = NL // TILE
    cols = width // 2
    whole = lambda i, *refs: (0, 0)
    return pl.pallas_call(
        functools.partial(columns_kernel, chunk * steps, jobs),
        grid_spec=pltpu.PrefetchScalarGridSpec(
            num_scalar_prefetch=4,
            grid=(steps,),
            in_specs=[
                pl.BlockSpec((owners, 4, own_rows, NZ), lambda i, *refs: (0, i, 0, 0)),
                pl.BlockSpec((NL, NL), whole),
                pl.BlockSpec((NL, NL), whole),
                pl.BlockSpec(memory_space=pl.ANY),
                pl.BlockSpec(memory_space=pl.ANY),
            ],
            out_specs=[
                pl.BlockSpec((count * each * 2, cols, NZ), lambda i, *refs: (0, 0, 0))
                for kind, which, count, base_row, each in jobs
            ],
            scratch_shapes=[
                pltpu.VMEM((2 * per_col, TILE, 2 * NZ), jnp.bfloat16),
                pltpu.VMEM((2 * per_col, TILE, 2 * NZ), jnp.float32),
                pltpu.VMEM((2, NL, 2 * NZ), jnp.bfloat16),
                pltpu.VMEM((2, 2 * TILE, NZ), jnp.float32),
                pltpu.VMEM((cols * 2 * NL, NZ), jnp.float32),
                pltpu.VMEM((DEPTH, TILE, TILE), jnp.bfloat16),
                pltpu.VMEM((DEPTH, 2 * TILE, NZ), jnp.bfloat16),
                pltpu.SemaphoreType.DMA((DEPTH,)),
                pltpu.SemaphoreType.DMA((DEPTH,)),
                pltpu.VMEM((8, NZ), jnp.float32),
            ],
        ),
        out_shape=[
            jax.ShapeDtypeStruct((count * each * 2, cols, NZ), jnp.bfloat16)
            for kind, which, count, base_row, each in jobs
        ],
        cost_estimate=pl.CostEstimate(
            flops=60000000000 // chunks, bytes_accessed=40000000 // chunks, transcendentals=0
        ),
    )(*plan, spectra, *tables, kernels, samples)


def image_kernel(crosses, where_ref, early_ref, near_ref, *rest):
    cross_refs = rest[: len(crosses)]
    maps_ref, cos_ref, sin_ref, own_ref, send_ref, map_scr, late = rest[len(crosses) :]
    coil_id = where_ref[0]
    pen_id = where_ref[1]
    cosine = cos_ref[...]
    sine = sin_ref[...]
    cols = early_ref.shape[3]
    count = early_ref.shape[0] * cols
    near = near_ref.shape[0]
    half = NL // 2
    parts = []
    for part in range(2):
        lanes = []
        for row in range(2):
            spot = slice(row * NZ, (row + 1) * NZ)
            lanes.append(early_ref[:, row, part].reshape(count, NZ))
            base = pl.multiple_of((pen_id & near) * cols, cols)
            late[part, pl.ds(base, near * cols), spot] = near_ref[:, row, part].reshape(
                near * cols, NZ
            )
            for which, cross_ref in zip(crosses, cross_refs):
                base = pl.multiple_of((pen_id ^ which) * cols, cols)
                late[part, pl.ds(base, cols), spot] = cross_ref[row, part]
        parts.append(jnp.concatenate([jnp.concatenate(lanes, 1), late[part]], 0))
    back_real = mxu(cosine, parts[0]) - mxu(sine, parts[1])
    back_imag = mxu(sine, parts[0]) + mxu(cosine, parts[1])
    for row in range(2):
        lanes = slice(row * NZ, (row + 1) * NZ)
        for which in range(2):
            rows = slice(which * half, (which + 1) * half)
            side = coil_id if which == 0 else 1 - coil_id
            map_scr[2 * row + which] = maps_ref[row, side].astype(jnp.float32)
            map_real = map_scr[2 * row + which, pl.ds(0, half, 2), :]
            map_imag = map_scr[2 * row + which, pl.ds(1, half, 2), :]
            real = back_real[rows, lanes]
            imag = back_imag[rows, lanes]
            term_real = map_real * real + map_imag * imag
            term_imag = map_real * imag - map_imag * real
            if which == 0:
                own_ref[row, 0] = term_real
                own_ref[row, 1] = term_imag
            else:
                send_ref[row, 0] = term_real.astype(jnp.bfloat16)
                send_ref[row, 1] = term_imag.astype(jnp.bfloat16)


def image_stage(where, early, near, crosses, across, maps, tables, base_row, early_row):
    each, _, cols = across[0].shape[:3]
    owners = early.shape[0]
    half = NL // 2
    base = base_row // 2
    early_base = early_row // 2
    whole = lambda i, *refs: (0, 0)
    return pl.pallas_call(
        functools.partial(image_kernel, crosses),
        grid_spec=pltpu.PrefetchScalarGridSpec(
            num_scalar_prefetch=1,
            grid=(each // 2,),
            in_specs=[
                pl.BlockSpec(
                    (owners, 2, 2, cols, NZ), lambda i, *refs: (0, early_base + i, 0, 0, 0)
                ),
                pl.BlockSpec(
                    (near.shape[0], 2, 2, cols, NZ), lambda i, *refs: (0, base + i, 0, 0, 0)
                ),
            ]
            + [pl.BlockSpec((2, 2, cols, NZ), lambda i, *refs: (i, 0, 0, 0)) for one in across]
            + [
                pl.BlockSpec((2, 2, NL, NZ), lambda i, *refs: (base + i, 0, 0, 0)),
                pl.BlockSpec((NL, NL), whole),
                pl.BlockSpec((NL, NL), whole),
            ],
            out_specs=[
                pl.BlockSpec((2, 2, half, NZ), lambda i, *refs: (i, 0, 0, 0)),
                pl.BlockSpec((2, 2, half, NZ), lambda i, *refs: (i, 0, 0, 0)),
            ],
            scratch_shapes=[
                pltpu.VMEM((4, NL, NZ), jnp.float32),
                pltpu.VMEM((2, owners * cols, 2 * NZ), jnp.bfloat16),
            ],
        ),
        out_shape=[
            jax.ShapeDtypeStruct((each, 2, half, NZ), jnp.float32),
            jax.ShapeDtypeStruct((each, 2, half, NZ), jnp.bfloat16),
        ],
        cost_estimate=pl.CostEstimate(
            flops=8 * each * NL * NL * NZ, bytes_accessed=each * 1200000, transcendentals=0
        ),
    )(where, early, near, *across, maps, *tables)


def sum_kernel(total_ref, own_ref, other_ref, out_ref):
    half = own_ref.shape[2]
    for row in range(own_ref.shape[0]):
        for part in range(2):
            rows = pl.ds(part, half, 2)
            out_ref[row, rows, :] = (
                total_ref[row, rows, :] + own_ref[row, part] + other_ref[row, part].astype(jnp.float32)
            )


def sum_stage(total, own, other, base_row):
    each, _, half = own.shape[:3]
    rows = 2
    base = base_row // rows
    return pl.pallas_call(
        sum_kernel,
        grid=(each // rows,),
        in_specs=[
            pl.BlockSpec((rows, 2 * half, NZ), lambda i: (base + i, 0, 0)),
            pl.BlockSpec((rows, 2, half, NZ), lambda i: (i, 0, 0, 0)),
            pl.BlockSpec((rows, 2, half, NZ), lambda i: (i, 0, 0, 0)),
        ],
        out_specs=pl.BlockSpec((rows, 2 * half, NZ), lambda i: (base + i, 0, 0)),
        out_shape=jax.ShapeDtypeStruct(total.shape, jnp.float32),
        input_output_aliases={0: 0},
        cost_estimate=pl.CostEstimate(
            flops=4 * each * half * NZ, bytes_accessed=each * 1000000, transcendentals=0
        ),
    )(total, own, other)


def block_plan(tile_of_block, pen_id, tile_count, group):
    count = tile_of_block.shape[0]
    local = tile_of_block - pen_id * tile_count
    spot = jnp.arange(count, dtype=jnp.int32)
    key = local * count + spot
    rank = jnp.sum((key[None, :] < key[:, None]).astype(jnp.int32), 1)
    hit = (rank[None, :] == spot[:, None]).astype(jnp.int32)
    order = jnp.sum(hit * spot[None, :], 1)
    sorted_tile = jnp.sum(hit * local[None, :], 1)
    edges = jnp.arange(tile_count // group + 1, dtype=jnp.int32) * group
    bounds = jnp.sum((local[None, :] < edges[:, None]).astype(jnp.int32), 1)
    return (order, sorted_tile % group, bounds)


def on_device_fast(*args):
    return gradient_parts(*args)


def gradient_parts(image_field, coil_maps, samples, kernels, tile_of_block):
    own_rows = image_field.shape[0]
    pen_count = lax.axis_size("pen")
    local_cols = NL // pen_count
    pen_id = lax.axis_index("pen")
    coil_id = lax.axis_index("coil")
    chunks = 2
    chunk_cols = local_cols // chunks
    image = image_field.reshape(own_rows, 2 * NL, NZ)
    maps = coil_maps.reshape(own_rows, 2 * NL, NZ)
    block_count = kernels.shape[0]
    sample_rows = samples.reshape(block_count, 2 * TILE, NZ)
    natural = numpy.arange(NL)
    split = (
        natural.reshape(pen_count, chunks, chunk_cols).transpose(1, 0, 2).reshape(NL)
    )
    tables_rows = pair_tables(1.0 / 16, split, natural)
    tables_cols = pair_tables(1.0 / 32, natural, natural)
    tables_back = pair_tables(1.0 / 16, natural, split)
    per_col = NL // TILE
    plan = block_plan(tile_of_block, pen_id, block_count // 2, 2 * per_col)

    def exchange(array):
        return lax.all_to_all(array, "pen", split_axis=0, concat_axis=0, tiled=True)

    above = shifted(image[-1:], "pen", 1)
    below = shifted(image[:1], "pen", -1)
    arrived = []
    for chunk in range(chunks):
        spectra = row_spectra(image, maps, tables_rows, chunk, chunks)
        spectra = spectra.reshape(pen_count, 2 * chunk_cols, own_rows, NZ)
        arrived.append(exchange(spectra))
    where = jnp.stack([coil_id, pen_id]).astype(jnp.int32)
    plan = plan + (where[1:],)
    unit = own_rows // 32
    sizes = [10 * unit, 10 * unit, 6 * unit, 6 * unit]
    row_pieces = tuple((sum(sizes[:n]), sizes[n]) for n in range(len(sizes)))
    near_count = pen_count // 2
    crosses = tuple(range(near_count, pen_count))
    near_groups = [list(range(near_count)), list(range(near_count, pen_count))]
    cut = sizes[0] + sizes[1]
    halves = ((0, cut), (cut, own_rows - cut))

    first = column_stage(
        arrived[0],
        tables_cols,
        kernels,
        sample_rows,
        plan,
        0,
        chunks,
        tuple(("all", 0, pen_count, base_row, each) for base_row, each in halves),
    )
    early = []
    for part, (base_row, each) in enumerate(halves):
        early.append(exchange(first[part].reshape(pen_count, each, 2, chunk_cols, NZ)))
    jobs = [("near", near_count, near_count, 0, own_rows)]
    for base_row, each in row_pieces:
        jobs += [("cross", which, 1, base_row, each) for which in crosses]
    result = column_stage(
        arrived[1], tables_cols, kernels, sample_rows, plan, 1, chunks, tuple(jobs)
    )
    near = lax.all_to_all(
        result[0].reshape(near_count, own_rows, 2, chunk_cols, NZ),
        "pen",
        split_axis=0,
        concat_axis=0,
        axis_index_groups=near_groups,
        tiled=True,
    )
    across = []
    for piece, (base_row, each) in enumerate(row_pieces):
        across.append(
            [
                lax.ppermute(
                    result[1 + piece * near_count + place].reshape(each, 2, chunk_cols, NZ),
                    "pen",
                    [(i, i ^ which) for i in range(pen_count)],
                )
                for place, which in enumerate(crosses)
            ]
        )
    shift = coil_id * (NL // 2)
    back_cos = jnp.roll(tables_back[0], -shift, 0)
    later_shift = lax.optimization_barrier((shift, result[-1]))[0]
    back_sin = jnp.roll(tables_back[1], -later_shift, 0)
    total = variation_stage(image, above, below, where)
    side_maps = maps.reshape(own_rows, 2, NL, NZ)
    for piece, (base_row, each) in enumerate(row_pieces):
        part = 0 if base_row < cut else 1
        own, send = image_stage(
            where,
            early[part],
            near,
            crosses,
            across[piece],
            side_maps,
            (back_cos, back_sin),
            base_row,
            base_row - halves[part][0],
        )
        other = lax.ppermute(send, "coil", [(0, 1), (1, 0)])
        total = sum_stage(total, own, other, base_row)
    return total.reshape(own_rows, NL // 2, 2, NZ)


def variation_kernel(where_ref, rows_ref, after_ref, above_ref, below_ref, out_ref, window, flux_y, flux_x):
    coil_id = where_ref[0]
    pen_id = where_ref[1]
    step = pl.program_id(0)
    steps = pl.num_programs(0)
    count = rows_ref.shape[0]
    half = out_ref.shape[1]
    offset = pl.multiple_of(coil_id * half, half)
    before = pl.multiple_of(jnp.maximum(offset - 8, 0), 8)
    behind = pl.multiple_of(jnp.minimum(offset + half, 2 * NL - 8), 8)
    lane = lax.broadcasted_iota(jnp.int32, (1, NZ), 1)
    not_last_plane = (lane != NZ - 1).astype(jnp.float32)

    def place(slot, ref, row):
        window[slot, pl.ds(0, 8), :] = ref[row, pl.ds(before, 8), :]
        window[slot, pl.ds(8, half), :] = ref[row, pl.ds(offset, half), :]
        window[slot, pl.ds(half + 8, 8), :] = ref[row, pl.ds(behind, 8), :]

    def flux(slot, next_slot, start, size, row_scale):
        center = window[slot, pl.ds(start, size), :]
        row = lax.broadcasted_iota(jnp.int32, (size, NZ), 0)
        column_row = row + (start - 8) + offset
        not_last = jnp.where(column_row < 2 * NL - 2, 1.0, 0.0)
        diff_y = (window[next_slot, pl.ds(start, size), :] - center) * row_scale
        diff_x = (window[slot, pl.ds(start + 2, size), :] - center) * not_last
        diff_z = (pltpu.roll(center, NZ - 1, 1) - center) * not_last_plane
        square = diff_y * diff_y + diff_x * diff_x + diff_z * diff_z
        split = square.reshape(size // 8, 8, NZ)
        up = pltpu.roll(split, 7, 1).reshape(size, NZ)
        down = pltpu.roll(split, 1, 1).reshape(size, NZ)
        square = square + jnp.where(row % 2 == 0, up, down)
        scale = lax.rsqrt(1.0 + square)
        return diff_y * scale, diff_x * scale, diff_z * scale

    size = half // 4

    @pl.when(step == 0)
    def _():
        place(1, above_ref, 0)
        place(0, rows_ref, 0)
        inside = jnp.where(pen_id > 0, 1.0, 0.0)

        def first(part, carry):
            start = pl.multiple_of(8 + part * size, 8)
            flux_y[pl.ds(start - 8, size), :] = flux(1, 0, start, size, 1.0)[0] * inside
            return carry

        lax.fori_loop(0, 4, first, 0)

    last_step = step == steps - 1
    last_pen = pen_id == lax.axis_size("pen") - 1

    def one_row(row, carry):
        slot = lax.rem(row, 2)
        is_end = row == count - 1

        @pl.when(jnp.logical_not(is_end))
        def _():
            place(1 - slot, rows_ref, jnp.minimum(row + 1, count - 1))

        @pl.when(jnp.logical_and(is_end, jnp.logical_not(last_step)))
        def _():
            place(1 - slot, after_ref, 0)

        @pl.when(jnp.logical_and(is_end, last_step))
        def _():
            place(1 - slot, below_ref, 0)

        row_scale = jnp.where(
            jnp.logical_and(jnp.logical_and(is_end, last_step), last_pen), 0.0, 1.0
        )
        edge = flux(slot, 1 - slot, 0, 8, row_scale)[1]
        flux_x[pl.ds(0, 8), :] = edge * jnp.where(coil_id > 0, 1.0, 0.0)

        def part_of(part, carry):
            start = pl.multiple_of(8 + part * size, 8)
            here_y, here_x, here_z = flux(slot, 1 - slot, start, size, row_scale)
            flux_x[pl.ds(start, size), :] = here_x
            past_y = flux_y[pl.ds(start - 8, size), :]
            flux_y[pl.ds(start - 8, size), :] = here_y
            past_x = flux_x[pl.ds(start - 2, size), :]
            past_z = pltpu.roll(here_z, 1, 1)
            total = (past_y - here_y) + (past_x - here_x) + (past_z - here_z)
            out_ref[row, pl.ds(start - 8, size), :] = tv_weight * total
            return carry

        lax.fori_loop(0, 4, part_of, 0)
        return carry

    lax.fori_loop(0, count, one_row, 0)


def variation_stage(image, above, below, where):
    rows = image.shape[0]
    count = 8
    return pl.pallas_call(
        variation_kernel,
        grid_spec=pltpu.PrefetchScalarGridSpec(
            num_scalar_prefetch=1,
            grid=(rows // count,),
            in_specs=[
                pl.BlockSpec((count, 2 * NL, NZ), lambda i, *refs: (i, 0, 0)),
                pl.BlockSpec(
                    (1, 2 * NL, NZ), lambda i, *refs: (jnp.minimum(count * (i + 1), rows - 1), 0, 0)
                ),
                pl.BlockSpec((1, 2 * NL, NZ), lambda i, *refs: (0, 0, 0)),
                pl.BlockSpec((1, 2 * NL, NZ), lambda i, *refs: (0, 0, 0)),
            ],
            out_specs=pl.BlockSpec((count, NL, NZ), lambda i, *refs: (i, 0, 0)),
            scratch_shapes=[
                pltpu.VMEM((2, NL + 16, NZ), jnp.float32),
                pltpu.VMEM((NL, NZ), jnp.float32),
                pltpu.VMEM((NL + 8, NZ), jnp.float32),
            ],
        ),
        out_shape=jax.ShapeDtypeStruct((rows, NL, NZ), jnp.float32),
        cost_estimate=pl.CostEstimate(
            flops=40 * rows * NL * NZ, bytes_accessed=60000000, transcendentals=0
        ),
        name="variation",
    )(where, image, image, above, below)


def solution(mesh):
    in_specs = (
        P("pen", None, None, None),
        P("coil", "pen", None, None, None),
        P("coil", "pen", None, None, None),
        P("pen", None, None),
        P("pen"),
    )
    out_specs = P("pen", "coil", None, None)
    own_rows = NL // mesh.shape["pen"]
    body = on_device_fast if own_rows % 32 == 0 else on_device
    return jax.shard_map(
        body, mesh=mesh, in_specs=in_specs, out_specs=out_specs, check_vma=False
    )
```

```python
import functools
import math

import numpy

import jax
import jax.numpy as jnp
from jax import lax
from jax.experimental import pallas as pl
from jax.experimental.pallas import tpu as pltpu

from jax.sharding import PartitionSpec as P

NL = 512
NZ = 128
TILE = 128


tv_weight = 2.0


def shifted(shard, axis, by):
    length = lax.axis_size(axis)
    pairs = [(i, i + by) for i in range(length) if 0 <= i + by < length]
    return lax.ppermute(shard, axis, pairs)


def dft_tables(length, direction):
    index = lax.iota(jnp.int32, length)
    phase = index[:, None] * index[None, :] % length
    angle = 2.0 * math.pi / length * phase.astype(jnp.float32)
    cosine = jnp.cos(angle) / math.sqrt(length)
    sine = direction * jnp.sin(angle) / math.sqrt(length)
    table = jnp.stack([jnp.stack([cosine, sine], -1), jnp.stack([-sine, cosine], -1)], 1)
    high_part = table.astype(jnp.bfloat16)
    low_part = (table - high_part.astype(jnp.float32)).astype(jnp.bfloat16)
    return (high_part, low_part)


def along_second(tables, values):
    first = jnp.einsum("kpxr,yxrz->ykpz", tables[0], values, preferred_element_type=jnp.float32)
    return first + jnp.einsum(
        "kpxr,yxrz->ykpz", tables[1], values, preferred_element_type=jnp.float32
    )


def along_first(tables, values):
    first = jnp.einsum("kpyr,yxrz->kxpz", tables[0], values, preferred_element_type=jnp.float32)
    return first + jnp.einsum(
        "kpyr,yxrz->kxpz", tables[1], values, preferred_element_type=jnp.float32
    )


def flux_fields(extended, first_row, first_col):
    center = extended[:-1, :-1]
    row_ids = first_row + jnp.arange(center.shape[0])
    col_ids = first_col + jnp.arange(center.shape[1])
    diff_y = (extended[1:, :-1] - center) * (row_ids != NL - 1)[:, None, None, None]
    diff_x = (extended[:-1, 1:] - center) * (col_ids != NL - 1)[None, :, None, None]
    diff_z = jnp.concatenate(
        [center[..., 1:] - center[..., :-1], jnp.zeros_like(center[..., :1])], 3
    )
    norm_den = jnp.sqrt(
        1.0 + jnp.sum(diff_y * diff_y + diff_x * diff_x + diff_z * diff_z, axis=2, keepdims=True)
    )
    inside = ((row_ids >= 0)[:, None] & (col_ids >= 0)[None, :]).astype(jnp.float32)[
        :, :, None, None
    ]
    return (diff_y / norm_den * inside, diff_x / norm_den * inside, diff_z / norm_den * inside)


def plane_divergence(flux_z):
    return jnp.concatenate([jnp.zeros_like(flux_z[..., :1]), flux_z[..., :-1]], 3) - flux_z


def on_device(image_field, coil_maps, samples, kernels, tile_of_block):
    own_rows = image_field.shape[0]
    pen_count = lax.axis_size("pen")
    half_cols = NL // lax.axis_size("coil")
    local_cols = NL // pen_count
    pen_id = lax.axis_index("pen")
    coil_id = lax.axis_index("coil")
    row_start = pen_id * own_rows
    col_start = coil_id * half_cols
    map_real = coil_maps[0, :, :, 0].astype(jnp.float32)
    map_imag = coil_maps[0, :, :, 1].astype(jnp.float32)
    field_real = image_field[:, :, 0]
    field_imag = image_field[:, :, 1]
    coil_image = jnp.stack(
        [
            map_real * field_real - map_imag * field_imag,
            map_real * field_imag + map_imag * field_real,
        ],
        2,
    ).astype(jnp.bfloat16)
    forward_tab = dft_tables(NL, 1.0)
    adjoint_tab = dft_tables(NL, -1.0)
    rows_spectrum = along_second(forward_tab, coil_image).astype(jnp.bfloat16)
    kspace_grid = along_first(
        forward_tab, lax.all_to_all(rows_spectrum, "pen", split_axis=1, concat_axis=0, tiled=True)
    ).astype(jnp.bfloat16)
    grid_tiles = (
        kspace_grid.reshape(NL // TILE, TILE, local_cols, 2 * NZ)
        .transpose(2, 0, 1, 3)
        .reshape(-1, TILE, 2 * NZ)
    )
    tile_count = grid_tiles.shape[0]
    local_ids = tile_of_block - pen_id * tile_count
    picked = jnp.take(grid_tiles, local_ids, axis=0)
    predicted = jnp.einsum("bst,btc->bsc", kernels, picked, preferred_element_type=jnp.float32)
    measured = samples[0].reshape(predicted.shape).astype(jnp.float32)
    misfit = (predicted - measured).astype(jnp.bfloat16)
    back_terms = jnp.einsum("bst,bsc->btc", kernels, misfit, preferred_element_type=jnp.float32)
    onehot = (local_ids[:, None] == jnp.arange(tile_count, dtype=jnp.int32)[None, :]).astype(
        jnp.float32
    )
    back_tiles = jnp.einsum(
        "bl,btc->ltc", onehot, back_terms, precision=lax.Precision.HIGHEST
    ).astype(jnp.bfloat16)
    back_grid = (
        back_tiles.reshape(local_cols, NL // TILE, TILE, 2 * NZ)
        .transpose(1, 2, 0, 3)
        .reshape(NL, local_cols, 2, NZ)
    )
    back_rows = along_first(adjoint_tab, back_grid).astype(jnp.bfloat16)
    back_image = along_second(
        adjoint_tab, lax.all_to_all(back_rows, "pen", split_axis=0, concat_axis=1, tiled=True)
    )
    back_real = back_image[:, :, 0]
    back_imag = back_image[:, :, 1]
    coil_term = jnp.stack(
        [map_real * back_real + map_imag * back_imag, map_real * back_imag - map_imag * back_real],
        2,
    )
    summed = lax.psum(coil_term, "coil")
    data_gradient = lax.dynamic_slice_in_dim(summed, col_start, half_cols, 1)
    padded = jnp.pad(image_field, ((0, 0), (1, 1), (0, 0), (0, 0)))
    window = lax.dynamic_slice_in_dim(padded, col_start, half_cols + 2, 1)
    upper_row = shifted(window[:1], "pen", -1)
    extended = jnp.concatenate([window, upper_row], 0)
    flux_y, flux_x, flux_z = flux_fields(extended, row_start, col_start - 1)
    lower_row = shifted(flux_y[-1:], "pen", 1)
    flux_before = jnp.concatenate([lower_row, flux_y[:-1]], 0)
    tv_part = (
        flux_before[:, 1:]
        - flux_y[:, 1:]
        + flux_x[:, :-1]
        - flux_x[:, 1:]
        + plane_divergence(flux_z[:, 1:])
    )
    return data_gradient + tv_weight * tv_part


PAD = 8


def pair_tables(scale, row_order, col_order):
    phase = numpy.outer(row_order, col_order) % NL
    angle = 2.0 * math.pi / NL * phase
    return (
        jnp.asarray(numpy.cos(angle) * scale, jnp.bfloat16),
        jnp.asarray(numpy.sin(angle) * scale, jnp.bfloat16),
    )


def mxu(left, right):
    return jnp.dot(left, right, preferred_element_type=jnp.float32)


def rows_kernel(image_ref, maps_ref, cos_ref, sin_ref, out_ref, map_scr, spec_scr):
    half = pl.program_id(1)
    out_rows = cos_ref.shape[0]
    stride = 2 * out_rows + PAD
    cosine = cos_ref[...]
    sine = sin_ref[...]
    for pair in range(4):
        reals, imags = [], []
        for row in (2 * pair, 2 * pair + 1):
            map_scr[row] = maps_ref[row].astype(jnp.float32)
            map_real = map_scr[row, pl.ds(0, NL, 2), :]
            map_imag = map_scr[row, pl.ds(1, NL, 2), :]
            field_real = image_ref[row, pl.ds(0, NL, 2), :]
            field_imag = image_ref[row, pl.ds(1, NL, 2), :]
            reals.append((map_real * field_real - map_imag * field_imag).astype(jnp.bfloat16))
            imags.append((map_real * field_imag + map_imag * field_real).astype(jnp.bfloat16))
        real = jnp.concatenate(reals, 1)
        imag = jnp.concatenate(imags, 1)
        spec_real = mxu(cosine, real) + mxu(sine, imag)
        spec_imag = mxu(cosine, imag) - mxu(sine, real)
        for sub in range(2):
            base = pl.multiple_of((half * 8 + 2 * pair + sub) * stride, 8)
            lanes = slice(sub * NZ, (sub + 1) * NZ)
            spec_scr[pl.ds(base, out_rows), :] = spec_real[:, lanes]
            spec_scr[pl.ds(base + out_rows, out_rows), :] = spec_imag[:, lanes]

    @pl.when(half == 1)
    def _():
        def move(step, carry):
            for sub in range(8):
                col = step * 8 + sub
                for part in range(2):
                    start = part * out_rows + col
                    low = spec_scr[pl.ds(start, 8, stride), :]
                    high = spec_scr[pl.ds(start + 8 * stride, 8, stride), :]
                    out_ref[2 * col + part] = jnp.concatenate([low, high], 0).astype(jnp.bfloat16)
            return carry

        lax.fori_loop(0, out_rows // 8, move, 0)


def row_spectra(image, maps, tables, chunk, chunks):
    rows = image.shape[0]
    out_rows = NL // chunks
    return pl.pallas_call(
        rows_kernel,
        grid=(rows // 16, 2),
        in_specs=[
            pl.BlockSpec((8, 2 * NL, NZ), lambda i, h: (2 * i + h, 0, 0)),
            pl.BlockSpec((8, 2 * NL, NZ), lambda i, h: (2 * i + h, 0, 0)),
            pl.BlockSpec((out_rows, NL), lambda i, h: (chunk, 0)),
            pl.BlockSpec((out_rows, NL), lambda i, h: (chunk, 0)),
        ],
        out_specs=pl.BlockSpec((2 * out_rows, 16, NZ), lambda i, h: (0, i, 0)),
        out_shape=jax.ShapeDtypeStruct((2 * out_rows, rows, NZ), jnp.bfloat16),
        scratch_shapes=[
            pltpu.VMEM((8, 2 * NL, NZ), jnp.float32),
            pltpu.VMEM((16 * (2 * out_rows + PAD), NZ), jnp.float32),
        ],
        cost_estimate=pl.CostEstimate(
            flops=8 * rows * out_rows * NL * NZ, bytes_accessed=30000000, transcendentals=0
        ),
    )(image, maps, *tables)


DEPTH = 8


def columns_kernel(
    first_group,
    jobs,
    order_ref,
    local_ref,
    bounds_ref,
    pen_ref,
    spec_ref,
    cos_ref,
    sin_ref,
    kernels_ref,
    samples_ref,
    *rest,
):
    out_count = len(jobs)
    outs = rest[:out_count]
    tiles, sums, backs, sample_scr, moved, kernel_buf, sample_buf, kernel_sem, sample_sem, _ = rest[
        out_count:
    ]
    step = pl.program_id(0)
    steps = pl.num_programs(0)
    first = bounds_ref[first_group]
    last = bounds_ref[first_group + steps]
    begin = bounds_ref[first_group + step]
    end = bounds_ref[first_group + step + 1]

    def fetch(place):
        slot = lax.rem(place, DEPTH)
        block = order_ref[place]
        return (
            pltpu.make_async_copy(kernels_ref.at[block], kernel_buf.at[slot], kernel_sem.at[slot]),
            pltpu.make_async_copy(samples_ref.at[block], sample_buf.at[slot], sample_sem.at[slot]),
        )

    def start(place):
        @pl.when(place < last)
        def _():
            for copy in fetch(place):
                copy.start()

    @pl.when(step == 0)
    def _():
        for ahead in range(DEPTH):
            start(first + ahead)

    cosine = cos_ref[...]
    sine = sin_ref[...]
    length = spec_ref.shape[0] * spec_ref.shape[2]
    parts = [
        jnp.concatenate([spec_ref[:, 2 * col + part].reshape(length, NZ) for col in range(2)], 1)
        for part in range(2)
    ]
    grid_real = (mxu(cosine, parts[0]) + mxu(sine, parts[1])).astype(jnp.bfloat16)
    grid_imag = (mxu(cosine, parts[1]) - mxu(sine, parts[0])).astype(jnp.bfloat16)
    per_col = NL // TILE
    for col in range(2):
        lanes = slice(col * NZ, (col + 1) * NZ)
        for tile in range(per_col):
            cells = slice(tile * TILE, (tile + 1) * TILE)
            tiles[col * per_col + tile, :, :NZ] = grid_real[cells, lanes]
            tiles[col * per_col + tile, :, NZ:] = grid_imag[cells, lanes]
    sums[...] = jnp.zeros_like(sums)

    def one(place, buf):
        slot = lax.rem(place, DEPTH)
        tile = local_ref[place]
        weights = kernel_buf[slot]
        predicted = mxu(weights, tiles[tile])
        sample_scr[buf] = sample_buf[slot].astype(jnp.float32)
        measured = jnp.concatenate(
            [sample_scr[buf, pl.ds(0, TILE, 2), :], sample_scr[buf, pl.ds(1, TILE, 2), :]], 1
        )
        misfit = (predicted - measured).astype(jnp.bfloat16)
        back = lax.dot_general(
            weights, misfit, (((0,), (0,)), ((), ())), preferred_element_type=jnp.float32
        )
        return tile, back

    def two(pair, carry):
        place = begin + 2 * pair
        other = jnp.minimum(place + 1, end - 1)
        for copy in fetch(place):
            copy.wait()

        @pl.when(place + 1 < end)
        def _():
            for copy in fetch(place + 1):
                copy.wait()

        tile_a, back_a = one(place, 0)
        tile_b, back_b = one(other, 1)
        sums[tile_a] += back_a
        sums[tile_b] += jnp.where(place + 1 < end, back_b, 0.0)
        start(place + DEPTH)

        @pl.when(place + 1 < end)
        def _():
            start(place + 1 + DEPTH)

        return carry

    lax.fori_loop(0, (end - begin + 1) // 2, two, 0)

    for col in range(2):
        lanes = slice(col * NZ, (col + 1) * NZ)
        for tile in range(per_col):
            cells = slice(tile * TILE, (tile + 1) * TILE)
            value = sums[col * per_col + tile].astype(jnp.bfloat16)
            backs[0, cells, lanes] = value[:, :NZ]
            backs[1, cells, lanes] = value[:, NZ:]
    back_real = backs[0]
    back_imag = backs[1]
    rows_real = mxu(cosine, back_real) - mxu(sine, back_imag)
    rows_imag = mxu(sine, back_real) + mxu(cosine, back_imag)
    for col in range(2):
        lanes = slice(col * NZ, (col + 1) * NZ)
        base = pl.multiple_of((2 * step + col) * (2 * NL + PAD), 8)
        moved[pl.ds(base, NL), :] = rows_real[:, lanes]
        moved[pl.ds(base + NL, NL), :] = rows_imag[:, lanes]

    @pl.when(step == steps - 1)
    def _():
        own_rows = spec_ref.shape[2]
        stride = 2 * NL + PAD
        groups = moved.shape[0] // (8 * stride)
        for out, (kind, which, count, base_row, each) in zip(outs, jobs):
            if kind == "cross":
                base_owner = pen_ref[0] ^ which
            elif kind == "near":
                base_owner = pen_ref[0] & which
            else:
                base_owner = 0

            def move(row, carry):
                owner = base_owner + row // each
                source = owner * own_rows + base_row + lax.rem(row, each)
                for part in range(2):
                    start_row = part * NL + source
                    out[2 * row + part] = jnp.concatenate(
                        [
                            moved[pl.ds(start_row + 8 * stride * group, 8, stride), :]
                            for group in range(groups)
                        ],
                        0,
                    ).astype(jnp.bfloat16)
                return carry

            lax.fori_loop(0, count * each, move, 0, unroll=2)


def column_stage(spectra, tables, kernels, samples, plan, chunk, chunks, jobs):
    owners, width, own_rows = spectra.shape[:3]
    steps = width // 4
    per_col = NL // TILE
    cols = width // 2
    whole = lambda i, *refs: (0, 0)
    return pl.pallas_call(
        functools.partial(columns_kernel, chunk * steps, jobs),
        grid_spec=pltpu.PrefetchScalarGridSpec(
            num_scalar_prefetch=4,
            grid=(steps,),
            in_specs=[
                pl.BlockSpec((owners, 4, own_rows, NZ), lambda i, *refs: (0, i, 0, 0)),
                pl.BlockSpec((NL, NL), whole),
                pl.BlockSpec((NL, NL), whole),
                pl.BlockSpec(memory_space=pl.ANY),
                pl.BlockSpec(memory_space=pl.ANY),
            ],
            out_specs=[
                pl.BlockSpec((count * each * 2, cols, NZ), lambda i, *refs: (0, 0, 0))
                for kind, which, count, base_row, each in jobs
            ],
            scratch_shapes=[
                pltpu.VMEM((2 * per_col, TILE, 2 * NZ), jnp.bfloat16),
                pltpu.VMEM((2 * per_col, TILE, 2 * NZ), jnp.float32),
                pltpu.VMEM((2, NL, 2 * NZ), jnp.bfloat16),
                pltpu.VMEM((2, 2 * TILE, NZ), jnp.float32),
                pltpu.VMEM((cols * (2 * NL + PAD), NZ), jnp.float32),
                pltpu.VMEM((DEPTH, TILE, TILE), jnp.bfloat16),
                pltpu.VMEM((DEPTH, 2 * TILE, NZ), jnp.bfloat16),
                pltpu.SemaphoreType.DMA((DEPTH,)),
                pltpu.SemaphoreType.DMA((DEPTH,)),
                pltpu.VMEM((8, NZ), jnp.float32),
            ],
        ),
        out_shape=[
            jax.ShapeDtypeStruct((count * each * 2, cols, NZ), jnp.bfloat16)
            for kind, which, count, base_row, each in jobs
        ],
        cost_estimate=pl.CostEstimate(
            flops=60000000000 // chunks, bytes_accessed=40000000 // chunks, transcendentals=0
        ),
    )(*plan, spectra, *tables, kernels, samples)


def image_kernel(where_ref, early_ref, *rest):
    owners = early_ref.shape[0]
    late_refs = rest[:owners]
    maps_ref, cos_ref, sin_ref, own_ref, send_ref, map_scr, late = rest[owners:]
    coil_id = where_ref[0]
    pen_id = where_ref[1]
    cosine = cos_ref[...]
    sine = sin_ref[...]
    cols = early_ref.shape[3]
    count = owners * cols
    half = NL // 2
    parts = []
    for part in range(2):
        lanes = []
        for row in range(2):
            spot = slice(row * NZ, (row + 1) * NZ)
            lanes.append(early_ref[:, row, part].reshape(count, NZ))
            for which, late_ref in enumerate(late_refs):
                base = pl.multiple_of((pen_id ^ which) * cols, cols)
                late[part, pl.ds(base, cols), spot] = late_ref[row, part]
        parts.append(jnp.concatenate([jnp.concatenate(lanes, 1), late[part]], 0))
    back_real = mxu(cosine, parts[0]) - mxu(sine, parts[1])
    back_imag = mxu(sine, parts[0]) + mxu(cosine, parts[1])
    for row in range(2):
        lanes = slice(row * NZ, (row + 1) * NZ)
        for which in range(2):
            rows = slice(which * half, (which + 1) * half)
            side = coil_id if which == 0 else 1 - coil_id
            map_scr[2 * row + which] = maps_ref[row, side].astype(jnp.float32)
            map_real = map_scr[2 * row + which, pl.ds(0, half, 2), :]
            map_imag = map_scr[2 * row + which, pl.ds(1, half, 2), :]
            real = back_real[rows, lanes]
            imag = back_imag[rows, lanes]
            term_real = map_real * real + map_imag * imag
            term_imag = map_real * imag - map_imag * real
            if which == 0:
                own_ref[row, 0] = term_real
                own_ref[row, 1] = term_imag
            else:
                send_ref[row, 0] = term_real.astype(jnp.bfloat16)
                send_ref[row, 1] = term_imag.astype(jnp.bfloat16)


def image_stage(where, early, across, maps, tables, base_row, early_row):
    each, _, cols = across[0].shape[:3]
    owners = early.shape[0]
    half = NL // 2
    base = base_row // 2
    early_base = early_row // 2
    whole = lambda i, *refs: (0, 0)
    return pl.pallas_call(
        image_kernel,
        grid_spec=pltpu.PrefetchScalarGridSpec(
            num_scalar_prefetch=1,
            grid=(each // 2,),
            in_specs=[
                pl.BlockSpec(
                    (owners, 2, 2, cols, NZ), lambda i, *refs: (0, early_base + i, 0, 0, 0)
                ),
            ]
            + [pl.BlockSpec((2, 2, cols, NZ), lambda i, *refs: (i, 0, 0, 0)) for one in across]
            + [
                pl.BlockSpec((2, 2, NL, NZ), lambda i, *refs: (base + i, 0, 0, 0)),
                pl.BlockSpec((NL, NL), whole),
                pl.BlockSpec((NL, NL), whole),
            ],
            out_specs=[
                pl.BlockSpec((2, 2, half, NZ), lambda i, *refs: (i, 0, 0, 0)),
                pl.BlockSpec((2, 2, half, NZ), lambda i, *refs: (i, 0, 0, 0)),
            ],
            scratch_shapes=[
                pltpu.VMEM((4, NL, NZ), jnp.float32),
                pltpu.VMEM((2, owners * cols, 2 * NZ), jnp.bfloat16),
            ],
        ),
        out_shape=[
            jax.ShapeDtypeStruct((each, 2, half, NZ), jnp.float32),
            jax.ShapeDtypeStruct((each, 2, half, NZ), jnp.bfloat16),
        ],
        cost_estimate=pl.CostEstimate(
            flops=8 * each * NL * NL * NZ, bytes_accessed=each * 1200000, transcendentals=0
        ),
    )(where, early, *across, maps, *tables)


def sum_kernel(total_ref, own_ref, other_ref, out_ref):
    half = own_ref.shape[2]
    for row in range(own_ref.shape[0]):
        for part in range(2):
            rows = pl.ds(part, half, 2)
            out_ref[row, rows, :] = (
                total_ref[row, rows, :] + own_ref[row, part] + other_ref[row, part].astype(jnp.float32)
            )


def sum_stage(total, own, other, base_row):
    each, _, half = own.shape[:3]
    rows = 2
    base = base_row // rows
    return pl.pallas_call(
        sum_kernel,
        grid=(each // rows,),
        in_specs=[
            pl.BlockSpec((rows, 2 * half, NZ), lambda i: (base + i, 0, 0)),
            pl.BlockSpec((rows, 2, half, NZ), lambda i: (i, 0, 0, 0)),
            pl.BlockSpec((rows, 2, half, NZ), lambda i: (i, 0, 0, 0)),
        ],
        out_specs=pl.BlockSpec((rows, 2 * half, NZ), lambda i: (base + i, 0, 0)),
        out_shape=jax.ShapeDtypeStruct(total.shape, jnp.float32),
        input_output_aliases={0: 0},
        cost_estimate=pl.CostEstimate(
            flops=4 * each * half * NZ, bytes_accessed=each * 1000000, transcendentals=0
        ),
    )(total, own, other)


def block_plan(tile_of_block, pen_id, tile_count, group):
    count = tile_of_block.shape[0]
    local = tile_of_block - pen_id * tile_count
    spot = jnp.arange(count, dtype=jnp.int32)
    key = local * count + spot
    rank = jnp.sum((key[None, :] < key[:, None]).astype(jnp.int32), 1)
    hit = (rank[None, :] == spot[:, None]).astype(jnp.int32)
    order = jnp.sum(hit * spot[None, :], 1)
    sorted_tile = jnp.sum(hit * local[None, :], 1)
    edges = jnp.arange(tile_count // group + 1, dtype=jnp.int32) * group
    bounds = jnp.sum((local[None, :] < edges[:, None]).astype(jnp.int32), 1)
    return (order, sorted_tile % group, bounds)


def on_device_fast(*args):
    return gradient_parts(*args)


def gradient_parts(image_field, coil_maps, samples, kernels, tile_of_block):
    own_rows = image_field.shape[0]
    pen_count = lax.axis_size("pen")
    local_cols = NL // pen_count
    pen_id = lax.axis_index("pen")
    coil_id = lax.axis_index("coil")
    chunks = 2
    chunk_cols = local_cols // chunks
    image = image_field.reshape(own_rows, 2 * NL, NZ)
    maps = coil_maps.reshape(own_rows, 2 * NL, NZ)
    block_count = kernels.shape[0]
    sample_rows = samples.reshape(block_count, 2 * TILE, NZ)
    natural = numpy.arange(NL)
    split = (
        natural.reshape(pen_count, chunks, chunk_cols).transpose(1, 0, 2).reshape(NL)
    )
    tables_rows = pair_tables(1.0 / 16, split, natural)
    tables_cols = pair_tables(1.0 / 32, natural, natural)
    tables_back = pair_tables(1.0 / 16, natural, split)
    per_col = NL // TILE
    plan = block_plan(tile_of_block, pen_id, block_count // 2, 2 * per_col)

    def exchange(array):
        return lax.all_to_all(array, "pen", split_axis=0, concat_axis=0, tiled=True)

    above = shifted(image[-1:], "pen", 1)
    below = shifted(image[:1], "pen", -1)
    arrived = []
    for chunk in range(chunks):
        spectra = row_spectra(image, maps, tables_rows, chunk, chunks)
        spectra = spectra.reshape(pen_count, 2 * chunk_cols, own_rows, NZ)
        arrived.append(exchange(spectra))
    where = jnp.stack([coil_id, pen_id]).astype(jnp.int32)
    plan = plan + (where[1:],)
    unit = own_rows // 32
    sizes = [10 * unit, 12 * unit, 6 * unit, 4 * unit]
    row_pieces = tuple((sum(sizes[:n]), sizes[n]) for n in range(len(sizes)))
    cut = sizes[0] + sizes[1]
    halves = ((0, cut), (cut, own_rows - cut))

    first = column_stage(
        arrived[0],
        tables_cols,
        kernels,
        sample_rows,
        plan,
        0,
        chunks,
        tuple(("all", 0, pen_count, base_row, each) for base_row, each in halves),
    )
    early = []
    for part, (base_row, each) in enumerate(halves):
        early.append(exchange(first[part].reshape(pen_count, each, 2, chunk_cols, NZ)))
    jobs = [
        ("cross", which, 1, base_row, each)
        for base_row, each in row_pieces
        for which in range(pen_count)
    ]
    result = column_stage(
        arrived[1], tables_cols, kernels, sample_rows, plan, 1, chunks, tuple(jobs)
    )
    across = []
    for piece, (base_row, each) in enumerate(row_pieces):
        ours = [
            one.reshape(each, 2, chunk_cols, NZ)
            for one in result[piece * pen_count : (piece + 1) * pen_count]
        ]
        for which in reversed(range(1, pen_count)):
            pairs = [(i, i ^ which) for i in range(pen_count)]
            ours[which] = lax.ppermute(ours[which], "pen", pairs)
        across.append(ours)
    shift = coil_id * (NL // 2)
    tables_back = [jnp.roll(table, -shift, 0) for table in tables_back]
    total = variation_stage(image, above, below, where)
    side_maps = maps.reshape(own_rows, 2, NL, NZ)
    for piece, (base_row, each) in enumerate(row_pieces):
        part = 0 if base_row < cut else 1
        own, send = image_stage(
            where,
            early[part],
            across[piece],
            side_maps,
            tables_back,
            base_row,
            base_row - halves[part][0],
        )
        other = lax.ppermute(send, "coil", [(0, 1), (1, 0)])
        total = sum_stage(total, own, other, base_row)
    return total.reshape(own_rows, NL // 2, 2, NZ)


def variation_kernel(where_ref, rows_ref, after_ref, above_ref, below_ref, out_ref, window, flux_y, flux_x):
    coil_id = where_ref[0]
    pen_id = where_ref[1]
    step = pl.program_id(0)
    steps = pl.num_programs(0)
    count = rows_ref.shape[0]
    half = out_ref.shape[1]
    offset = pl.multiple_of(coil_id * half, half)
    before = pl.multiple_of(jnp.maximum(offset - 8, 0), 8)
    behind = pl.multiple_of(jnp.minimum(offset + half, 2 * NL - 8), 8)
    lane = lax.broadcasted_iota(jnp.int32, (1, NZ), 1)
    not_last_plane = (lane != NZ - 1).astype(jnp.float32)

    def place(slot, ref, row):
        window[slot, pl.ds(0, 8), :] = ref[row, pl.ds(before, 8), :]
        window[slot, pl.ds(8, half), :] = ref[row, pl.ds(offset, half), :]
        window[slot, pl.ds(half + 8, 8), :] = ref[row, pl.ds(behind, 8), :]

    def flux(slot, next_slot, start, size, row_scale):
        center = window[slot, pl.ds(start, size), :]
        row = lax.broadcasted_iota(jnp.int32, (size, NZ), 0)
        column_row = row + (start - 8) + offset
        not_last = jnp.where(column_row < 2 * NL - 2, 1.0, 0.0)
        diff_y = (window[next_slot, pl.ds(start, size), :] - center) * row_scale
        diff_x = (window[slot, pl.ds(start + 2, size), :] - center) * not_last
        diff_z = (pltpu.roll(center, NZ - 1, 1) - center) * not_last_plane
        square = diff_y * diff_y + diff_x * diff_x + diff_z * diff_z
        split = square.reshape(size // 8, 8, NZ)
        up = pltpu.roll(split, 7, 1).reshape(size, NZ)
        down = pltpu.roll(split, 1, 1).reshape(size, NZ)
        square = square + jnp.where(row % 2 == 0, up, down)
        scale = lax.rsqrt(1.0 + square)
        return diff_y * scale, diff_x * scale, diff_z * scale

    size = half // 4

    @pl.when(step == 0)
    def _():
        place(1, above_ref, 0)
        place(0, rows_ref, 0)
        inside = jnp.where(pen_id > 0, 1.0, 0.0)

        def first(part, carry):
            start = pl.multiple_of(8 + part * size, 8)
            flux_y[pl.ds(start - 8, size), :] = flux(1, 0, start, size, 1.0)[0] * inside
            return carry

        lax.fori_loop(0, 4, first, 0)

    last_step = step == steps - 1
    last_pen = pen_id == lax.axis_size("pen") - 1

    def one_row(row, carry):
        slot = lax.rem(row, 2)
        is_end = row == count - 1

        @pl.when(jnp.logical_not(is_end))
        def _():
            place(1 - slot, rows_ref, jnp.minimum(row + 1, count - 1))

        @pl.when(jnp.logical_and(is_end, jnp.logical_not(last_step)))
        def _():
            place(1 - slot, after_ref, 0)

        @pl.when(jnp.logical_and(is_end, last_step))
        def _():
            place(1 - slot, below_ref, 0)

        row_scale = jnp.where(
            jnp.logical_and(jnp.logical_and(is_end, last_step), last_pen), 0.0, 1.0
        )
        edge = flux(slot, 1 - slot, 0, 8, row_scale)[1]
        flux_x[pl.ds(0, 8), :] = edge * jnp.where(coil_id > 0, 1.0, 0.0)

        def part_of(part, carry):
            start = pl.multiple_of(8 + part * size, 8)
            here_y, here_x, here_z = flux(slot, 1 - slot, start, size, row_scale)
            flux_x[pl.ds(start, size), :] = here_x
            past_y = flux_y[pl.ds(start - 8, size), :]
            flux_y[pl.ds(start - 8, size), :] = here_y
            past_x = flux_x[pl.ds(start - 2, size), :]
            past_z = pltpu.roll(here_z, 1, 1)
            total = (past_y - here_y) + (past_x - here_x) + (past_z - here_z)
            out_ref[row, pl.ds(start - 8, size), :] = tv_weight * total
            return carry

        lax.fori_loop(0, 4, part_of, 0)
        return carry

    lax.fori_loop(0, count, one_row, 0)


def variation_stage(image, above, below, where):
    rows = image.shape[0]
    count = 8
    return pl.pallas_call(
        variation_kernel,
        grid_spec=pltpu.PrefetchScalarGridSpec(
            num_scalar_prefetch=1,
            grid=(rows // count,),
            in_specs=[
                pl.BlockSpec((count, 2 * NL, NZ), lambda i, *refs: (i, 0, 0)),
                pl.BlockSpec(
                    (1, 2 * NL, NZ), lambda i, *refs: (jnp.minimum(count * (i + 1), rows - 1), 0, 0)
                ),
                pl.BlockSpec((1, 2 * NL, NZ), lambda i, *refs: (0, 0, 0)),
                pl.BlockSpec((1, 2 * NL, NZ), lambda i, *refs: (0, 0, 0)),
            ],
            out_specs=pl.BlockSpec((count, NL, NZ), lambda i, *refs: (i, 0, 0)),
            scratch_shapes=[
                pltpu.VMEM((2, NL + 16, NZ), jnp.float32),
                pltpu.VMEM((NL, NZ), jnp.float32),
                pltpu.VMEM((NL + 8, NZ), jnp.float32),
            ],
        ),
        out_shape=jax.ShapeDtypeStruct((rows, NL, NZ), jnp.float32),
        cost_estimate=pl.CostEstimate(
            flops=40 * rows * NL * NZ, bytes_accessed=60000000, transcendentals=0
        ),
        name="variation",
    )(where, image, image, above, below)


def solution(mesh):
    in_specs = (
        P("pen", None, None, None),
        P("coil", "pen", None, None, None),
        P("coil", "pen", None, None, None),
        P("pen", None, None),
        P("pen"),
    )
    out_specs = P("pen", "coil", None, None)
    own_rows = NL // mesh.shape["pen"]
    body = on_device_fast if own_rows % 32 == 0 else on_device
    return jax.shard_map(
        body, mesh=mesh, in_specs=in_specs, out_specs=out_specs, check_vma=False
    )
```
